32 devices in a mesh: shard: 8 (over z, y), tensor: 4 (over x, core).
Axes of the slice: x: 2, y: 2, z: 4, core: 2. Of those that a mesh axis runs over, the one named last changes fastest.
Arguments:
- grad_parts: float32 [4, 4, 768, 768], P('tensor', None, 'shard'), may hold values from -0.6 to 0.6
- adam_v: float32 [4, 768, 768], P(None, 'shard', 'tensor'), may hold values from 0.01 to 0.2
- left_stat: float32 [8, 768, 768], P('shard', 'tensor'), may hold values from -6 to 6
- right_stat: float32 [8, 768, 768], P('shard', 'tensor'), may hold values from -6 to 6
- left_root: bfloat16 [8, 768, 768], P('shard', 'tensor'), as said below
- right_root: bfloat16 [8, 768, 768], P('shard', 'tensor'), as said below
- owner: int32 [4], replicated, may hold values from 0 to 7, as said below
- vec_parts: float32 [4, 4, 768], P('tensor', None, 'shard'), may hold values from -0.6 to 0.6
- vec_m: float32 [4, 768], P(None, 'shard'), may hold values from -0.3 to 0.3
- vec_v: float32 [4, 768], P(None, 'shard'), may hold values from 0.01 to 0.2
Outputs:
- update: float32 [4, 768, 768], P(None, 'shard', 'tensor')
- new_adam_v: float32 [4, 768, 768], P(None, 'shard', 'tensor')
- new_left: float32 [8, 768, 768], P('shard', 'tensor')
- new_right: float32 [8, 768, 768], P('shard', 'tensor')
- new_vec_m: float32 [4, 768], P(None, 'shard')
- new_vec_v: float32 [4, 768], P(None, 'shard')
- vec_step: float32 [4, 768], P(None, 'shard')
The draws below stay inside these ranges and needn't reach their ends.
Inputs may be any that keep to these rules, and one draw needn't show every extreme that they name: owner holds 4 distinct slot numbers: no slot owns two tiles. `left_root`: each slot's matrix is symmetric. `right_root`: each slot's matrix is symmetric.
All inputs are finite; a program needn't handle non-finite values.
Results may differ from the reference program's by a relative error of at most 0.0003.
Values may be sent and summed in bfloat16 or wider, within the bound.
No kernel may reach another device: no remote copies, remote signals or barrier semaphores. Data moves between devices by JAX's collectives and lax.ppermute only.
A program may use at most 64 MiB of HBM per device.

```python
import math
import jax
import jax.numpy as jnp
from jax import lax

D = 768
MICRO = 4
TILES = 4
N_SHARD = 8


def symmetric_root(key):
    base = jax.random.normal(key, (N_SHARD, D, D), jnp.float32)
    mirrored = (base + jnp.swapaxes(base, 1, 2)) * (0.5 / math.sqrt(D))
    return (mirrored + jnp.eye(D, dtype=jnp.float32)[None, :, :]).astype(jnp.bfloat16)


def draw_left_root(key, part):
    return symmetric_root(jax.random.fold_in(key, 11))


def draw_right_root(key, part):
    return symmetric_root(jax.random.fold_in(key, 23))


def draw_owner(key, part):
    middle = jax.random.permutation(jax.random.fold_in(key, 5), N_SHARD - 2).astype(jnp.int32) + 1
    ends = jnp.array([0, N_SHARD - 1], dtype=jnp.int32)
    chosen = jnp.concatenate([ends, middle[:TILES - 2]])
    placed = jax.random.permutation(jax.random.fold_in(key, 7), chosen)
    return placed.astype(jnp.int32)


def level_of(rng, dims, split, smallest, top_value):
    def one(dim, blocks):
        draws = jax.random.uniform(jax.random.fold_in(jax.random.fold_in(rng, 6), dim), (blocks,), jnp.float32, smallest / len(split), top_value / len(split))
        return jnp.repeat(jnp.exp(draws), dims[dim] // blocks).reshape((-1,) + (1,) * (len(dims) - dim - 1))

    level = one(*split[0])
    for cut in split[1:]:
        level = level * one(*cut)
    return level


def noise(stream_key, shape, spread, most, pieces=(), kind=jnp.bfloat16):
    level = level_of(stream_key, shape, pieces, -0.22, 0.18) if pieces else 1.0
    result = jax.random.normal(stream_key, shape, jnp.float32) * spread * level
    return jnp.minimum(jnp.maximum(result, -most), most).astype(kind)


def setup_inputs(seed: int = 0) -> dict:
    splits = jax.random.split(jax.random.key(seed), 11)
    return {
        "grad_parts": noise(splits[0], (MICRO, TILES, D, D), 0.1, 0.6, ((0, 4), (2, 8)), jnp.float32),
        "adam_v": jnp.clip(jnp.exp(math.log(0.2) - 2.9957323 * jax.random.uniform(splits[1], (TILES, D, D), jnp.float32) ** level_of(splits[1], (TILES, D, D), ((1, 8), (2, 4)), -0.2, 0.2)), 0.01, 0.2),
        "left_stat": noise(splits[2], (N_SHARD, D, D), 1.0, 6.0, ((0, 8), (1, 4)), jnp.float32),
        "right_stat": noise(splits[3], (N_SHARD, D, D), 1.0, 6.0, ((0, 8), (1, 4)), jnp.float32),
        "left_root": draw_left_root(jax.random.fold_in(splits[10], 71), 0),
        "right_root": draw_right_root(jax.random.fold_in(splits[10], 71), 0),
        "owner": draw_owner(jax.random.fold_in(splits[10], 71), 0),
        "vec_parts": noise(splits[7], (MICRO, TILES, D), 0.1, 0.6, ((0, 4), (2, 8)), jnp.float32),
        "vec_m": noise(splits[8], (TILES, D), 0.05, 0.3, ((1, 8),), jnp.float32),
        "vec_v": jnp.clip(jnp.exp(math.log(0.2) - 2.9957323 * jax.random.uniform(splits[9], (TILES, D), jnp.float32) ** level_of(splits[9], (TILES, D), ((1, 8),), -0.2, 0.2)), 0.01, 0.2),
    }


BETA_ONE = 0.9
BETA_TWO = 0.95
STAT_DECAY = 0.95
STEP_COUNT = 10.0
EPSILON = 1e-08
NORM_EPS = 1e-06
HIGH = lax.Precision.HIGHEST

def reference(grad_parts, adam_v, left_stat, right_stat, left_root, right_root, owner, vec_parts, vec_m, vec_v):
    grad = lax.optimization_barrier(jnp.sum(grad_parts, axis=0))
    new_adam_v = BETA_TWO * adam_v + (1.0 - BETA_TWO) * grad * grad
    bias_two = 1.0 - BETA_TWO ** STEP_COUNT
    adam_dir = grad / (jnp.sqrt(new_adam_v / bias_two) + EPSILON)
    adam_sq = lax.optimization_barrier(jnp.sum(adam_dir * adam_dir, axis=(1, 2)))
    slot_hot = (jnp.arange(N_SHARD, dtype=jnp.int32)[:, None] == owner[None, :]).astype(jnp.float32)

    def refresh(items):
        hot_row, left_old, right_old = items
        tile = jnp.tensordot(hot_row, grad, axes=1, precision=HIGH)
        left_new = STAT_DECAY * left_old + (1.0 - STAT_DECAY) * jnp.dot(tile, tile.T, precision=HIGH)
        right_new = STAT_DECAY * right_old + (1.0 - STAT_DECAY) * jnp.dot(tile.T, tile, precision=HIGH)
        return (left_new, right_new)
    new_left, new_right = lax.map(refresh, (slot_hot, left_stat, right_stat))

    def precondition(items):
        tile, slot = items
        left_inv = lax.dynamic_index_in_dim(left_root, slot, 0, keepdims=False).astype(jnp.float32)
        right_inv = lax.dynamic_index_in_dim(right_root, slot, 0, keepdims=False).astype(jnp.float32)
        return jnp.dot(jnp.dot(left_inv, tile, precision=HIGH), right_inv, precision=HIGH)
    shampoo_dir = lax.map(precondition, (grad, owner))
    shampoo_sq = lax.optimization_barrier(jnp.sum(shampoo_dir * shampoo_dir, axis=(1, 2)))
    graft = jnp.sqrt(adam_sq) / (jnp.sqrt(shampoo_sq) + NORM_EPS)
    update = graft[:, None, None] * shampoo_dir
    vec_grad = lax.optimization_barrier(jnp.sum(vec_parts, axis=0))
    new_vec_m = BETA_ONE * vec_m + (1.0 - BETA_ONE) * vec_grad
    new_vec_v = BETA_TWO * vec_v + (1.0 - BETA_TWO) * vec_grad * vec_grad
    bias_one = 1.0 - BETA_ONE ** STEP_COUNT
    vec_step = new_vec_m / bias_one / (jnp.sqrt(new_vec_v / bias_two) + EPSILON)
    return (update, new_adam_v, new_left, new_right, new_vec_m, new_vec_v, vec_step)
```

```python
import functools

import jax
import jax.numpy as jnp
from jax import lax
from jax.experimental import pallas as pl
from jax.experimental.pallas import tpu as pltpu
from jax.sharding import PartitionSpec as P

BETA_ONE = 0.9
BETA_TWO = 0.95
STAT_DECAY = 0.95
STEP_COUNT = 10.0
EPSILON = 1e-08
NORM_EPS = 1e-06
BIAS_ONE = 1.0 - BETA_ONE**STEP_COUNT
BIAS_TWO = 1.0 - BETA_TWO**STEP_COUNT
HIGH = lax.Precision.HIGHEST
LANES = 128
EXTRA = 8
F32 = jnp.float32
BF16 = jnp.bfloat16


def plain(
    grad_parts, adam_v, left_stat, right_stat, left_root, right_root, owner, vec_parts, vec_m, vec_v
):
    shards = lax.axis_size("shard")
    tiles = owner.shape[0]
    grad = lax.psum_scatter(grad_parts[0], "tensor", scatter_dimension=2, tiled=True)
    rows_dev = grad.shape[1]
    cols_dev = grad.shape[2]
    new_adam_v = BETA_TWO * adam_v + (1.0 - BETA_TWO) * grad * grad
    adam_dir = grad / (jnp.sqrt(new_adam_v / BIAS_TWO) + EPSILON)
    adam_sq = jnp.sum(adam_dir * adam_dir, axis=(1, 2))
    vec_grad = lax.psum(vec_parts[0], "tensor")
    new_vec_m, new_vec_v, vec_step = vec_update(vec_grad, vec_m, vec_v)
    slot_hot = (jnp.arange(shards, dtype=jnp.int32)[:, None] == owner[None, :]).astype(F32)
    outgoing = jnp.dot(slot_hot, grad.reshape(tiles, rows_dev * cols_dev), precision=HIGH)
    outgoing = outgoing.reshape(shards, rows_dev, cols_dev)
    arrived = lax.all_to_all(outgoing, "shard", split_axis=0, concat_axis=1, tiled=True)[0]
    whole = lax.all_gather(arrived, "tensor", axis=1, tiled=True)
    start = lax.axis_index("tensor") * cols_dev
    tile_rows = lax.dynamic_slice_in_dim(whole, start, cols_dev, 0)
    new_left = STAT_DECAY * left_stat[0] + (1.0 - STAT_DECAY) * jnp.dot(
        tile_rows, whole.T, precision=HIGH
    )
    new_right = STAT_DECAY * right_stat[0] + (1.0 - STAT_DECAY) * jnp.dot(
        arrived.T, whole, precision=HIGH
    )
    left_full = lax.all_gather(left_root[0], "tensor", axis=0, tiled=True).astype(F32)
    right_part = jnp.dot(whole, right_root[0].astype(F32).T, precision=HIGH)
    direction = jnp.dot(left_full, right_part, precision=HIGH)
    returned = lax.all_to_all(
        direction.reshape(shards, rows_dev, cols_dev),
        "shard",
        split_axis=0,
        concat_axis=0,
        tiled=True,
    )
    update = jnp.dot(slot_hot.T, returned.reshape(shards, rows_dev * cols_dev), precision=HIGH)
    update = update.reshape(tiles, rows_dev, cols_dev)
    shampoo_local = jnp.sum(update * update, axis=(1, 2))
    adam_total, shampoo_total = lax.psum((adam_sq, shampoo_local), ("shard", "tensor"))
    graft = jnp.sqrt(adam_total) / (jnp.sqrt(shampoo_total) + NORM_EPS)
    update = graft[:, None, None] * update
    return (update, new_adam_v, new_left[None], new_right[None], new_vec_m, new_vec_v, vec_step)


def vec_update(vec_grad, vec_m, vec_v):
    new_vec_m = BETA_ONE * vec_m + (1.0 - BETA_ONE) * vec_grad
    new_vec_v = BETA_TWO * vec_v + (1.0 - BETA_TWO) * vec_grad * vec_grad
    vec_step = new_vec_m / BIAS_ONE / (jnp.sqrt(new_vec_v / BIAS_TWO) + EPSILON)
    return new_vec_m, new_vec_v, vec_step


def place():
    t = lax.axis_index("tensor")
    return lax.axis_index("shard"), t, t // 2, lax.rem(t, 2)


def lane_tile(index):
    return pl.ds(pl.multiple_of(index * LANES, LANES), LANES)


def swap_halves(a):
    return pltpu.roll(a, LANES // 2, 1)


def low_lanes(rows):
    return lax.broadcasted_iota(jnp.int32, (rows, LANES), 1) < LANES // 2


def fold(mid, core):
    half = mid.shape[0] // 2
    turned = swap_halves(mid)
    first = core == 0
    low = low_lanes(half)
    top = jnp.where(first, mid[:half], turned[:half])
    bottom = jnp.where(first, turned[half:], mid[half:])
    return jnp.where(low, top, bottom)


def unfold(block, rows, core):
    main, side = block[:rows], block[rows:]
    wide = jnp.concatenate([side, swap_halves(side)], axis=0)
    turned = swap_halves(main)
    first = core == 0
    head = jnp.where(first, main, jnp.where(low_lanes(rows), wide, turned))
    return head, jnp.where(first, wide, turned)[:, : LANES // 2]


def split_kernel(rows, tiles, g_ref, vec_ref, sf_ref, sn_ref, kf_ref, kn_ref):
    _, _, chip, core = place()
    packed = rows + rows // 2
    for out, far, own in ((sf_ref, True, False), (sn_ref, False, False), (kf_ref, True, True), (kn_ref, False, True)):
        x = 1 - chip if far else chip
        d = core if own else 1 - core
        for k in range(tiles):
            base = k * packed
            out[base : base + rows] = g_ref[0, k, :, lane_tile(3 * x + 2 * d)]
            out[base + rows : base + packed] = fold(g_ref[0, k, :, lane_tile(3 * x + 1)], d)
        if far:
            out[tiles * packed :] = jnp.zeros((EXTRA, LANES), F32)
            out[tiles * packed : tiles * packed + tiles, : rows] = vec_ref[0]


def tile_of(owner_ref, slot, tiles):
    k = jnp.int32(0)
    for i in range(1, tiles):
        k = jnp.where(owner_ref[i] == slot, i, k)
    return k


def adam_kernel(
    rows, tiles, shards, owner_ref, kn_ref, rn_ref, u_ref, r_ref, v_ref, m_ref, vv_ref, *refs
):
    outs, (nv_ref, vm_ref, vn_ref, vs_ref), (g_ref, ext_ref) = refs[:shards], refs[shards : shards + 4], refs[shards + 4 :]
    shard, _, _, core = place()
    packed = rows + rows // 2

    def one(g, v_old):
        v_new = BETA_TWO * v_old + (1.0 - BETA_TWO) * g * g
        step = g / (jnp.sqrt(v_new / BIAS_TWO) + EPSILON)
        sq = step * step
        return v_new, jnp.sum(sq.reshape(-1, 8, sq.shape[1]), axis=0)

    for k in range(tiles):
        at = slice(k * packed, k * packed + packed)
        g = kn_ref[at] + rn_ref[at] + r_ref[at]
        g_ref[k] = g
        head, tail = unfold(g, rows, core)
        nv_ref[k, :, :LANES], ext_ref[k] = one(head, v_ref[k, :, :LANES])
        nv_ref[k, :, LANES:], sq = one(tail, v_ref[k, :, LANES:])
        ext_ref[k, :, : LANES // 2] += sq
    for j in range(shards):
        k = tile_of(owner_ref, shard ^ j, tiles)
        outs[j][:packed] = g_ref[k]
        outs[j][packed:] = ext_ref[k]
    vec = u_ref[:tiles, :rows] + r_ref[tiles * packed : tiles * packed + tiles, :rows]
    vm_ref[...], vn_ref[...], vs_ref[...] = vec_update(vec, m_ref[...], vv_ref[...])


def roots_kernel(own_ref, core_ref, chip_ref, both_ref, left_ref, right_ref):
    _, t, _, _ = place()
    rows = own_ref.shape[1]
    for mask, ref in enumerate((own_ref, core_ref, chip_ref, both_ref)):
        at = pl.ds(pl.multiple_of((t ^ mask) * rows, rows), rows)
        left_ref[at, :] = ref[0]
        right_ref[at, :] = ref[1]


def halves(a):
    high = a.astype(BF16)
    return high, (a - high.astype(F32)).astype(BF16)


def owner_kernel(rows, shards, *refs):
    pieces, refs = refs[:8], refs[8:]
    left_ref, right_ref, refs = refs[0], refs[1], refs[2:]
    outs, (gh_ref, gl_ref), (zh_ref, zl_ref, dir_ref) = refs[:shards], refs[shards : shards + 2], refs[shards + 2 :]
    shard, _, chip, core = place()
    packed = rows + rows // 2
    half = rows // 2
    group = shards // 2
    low = low_lanes(half)
    adam = jnp.zeros((EXTRA, LANES), F32)
    for g in range(2):
        own, other = pieces[4 * g : 4 * g + 2], pieces[4 * g + 2 : 4 * g + 4]
        for i in range(group):
            to = pl.ds(pl.multiple_of((shard ^ (g * group + i)) * rows, rows), rows)
            base = i * (packed + EXTRA)
            for x, (mine, peer) in ((chip, own), (1 - chip, other)):
                a, b = mine[base : base + packed], peer[base : base + packed]
                adam += mine[base + packed : base + packed + EXTRA]
                adam += peer[base + packed : base + packed + EXTRA]
                first, last = jnp.where(core == 0, a, b), jnp.where(core == 0, b, a)
                fs, ls = first[rows:], last[rows:]
                mid = jnp.concatenate(
                    [
                        jnp.where(low, fs, swap_halves(ls)),
                        jnp.where(low, swap_halves(fs), ls),
                    ],
                    axis=0,
                )
                for n, tile in enumerate((first[:rows], mid, last[:rows])):
                    gh_ref[to, lane_tile(3 * x + n)], gl_ref[to, lane_tile(3 * x + n)] = halves(tile)
    size = gh_ref.shape[0]
    step = 256

    def right(i, carry):
        at = pl.ds(pl.multiple_of(i * step, step), step)
        z = jnp.dot(gh_ref[at, :], right_ref[...], preferred_element_type=F32)
        z += jnp.dot(gl_ref[at, :], right_ref[...], preferred_element_type=F32)
        zh_ref[at, :], zl_ref[at, :] = halves(z)
        return carry

    lax.fori_loop(0, size // step, right, 0)

    def left(i, total):
        at = pl.ds(pl.multiple_of(i * step, step), step)
        d = jnp.dot(left_ref[at, :], zh_ref[...], preferred_element_type=F32)
        d += jnp.dot(left_ref[at, :], zl_ref[...], preferred_element_type=F32)
        dir_ref[at, :] = d
        return total + jnp.sum((d * d).reshape(-1, 8, size), axis=0)

    squares = lax.fori_loop(0, size // step, left, jnp.zeros((8, size), F32))

    def whole(a):
        return jnp.sum(jnp.sum(a, axis=1, keepdims=True), axis=0, keepdims=True)

    graft = jnp.sqrt(whole(adam)) / (jnp.sqrt(whole(squares)) + NORM_EPS)
    for j in range(shards):
        at = pl.ds(pl.multiple_of((shard ^ j) * rows, rows), rows)
        outs[j][:rows] = graft * dir_ref[at, lane_tile(3 * chip + 2 * core)]
        outs[j][rows:] = graft * fold(dir_ref[at, lane_tile(3 * chip + 1)], core)


def stats_kernel(tiles, owner_ref, gh_ref, gl_ref, left_ref, right_ref, nl_ref, nr_ref):
    shard, t, chip, core = place()
    rows = left_ref.shape[1]
    held = owner_ref[0] == shard
    for i in range(1, tiles):
        held = jnp.logical_or(held, owner_ref[i] == shard)

    def product(high, low, dims):
        dot = functools.partial(lax.dot_general, dimension_numbers=(dims, ((), ())), preferred_element_type=F32)
        return dot(high, gh_ref[...]) + dot(high, gl_ref[...]) + dot(low, gh_ref[...])

    def refreshed(old, new):
        return STAT_DECAY * old + (1.0 - STAT_DECAY) * jnp.where(held, new, 0.0)

    at = pl.ds(pl.multiple_of(t * rows, rows), rows)
    nl_ref[0] = refreshed(left_ref[0], product(gh_ref[at, :], gl_ref[at, :], ((1,), (1,))))
    end, mid = lane_tile(3 * chip + 2 * core), lane_tile(3 * chip + 1)
    ends = product(gh_ref[:, end], gl_ref[:, end], ((0,), (0,)))
    mids = product(gh_ref[:, mid], gl_ref[:, mid], ((0,), (0,)))
    half = LANES // 2

    @pl.when(core == 0)
    def _():
        nr_ref[0, :LANES] = refreshed(right_ref[0, :LANES], ends)
        nr_ref[0, LANES:] = refreshed(right_ref[0, LANES:], mids[:half])

    @pl.when(core == 1)
    def _():
        nr_ref[0, :half] = refreshed(right_ref[0, :half], mids[half:])
        nr_ref[0, half:] = refreshed(right_ref[0, half:], ends)


def back_kernel(rows, tiles, shards, owner_ref, *refs):
    blocks, out_ref = refs[:shards], refs[shards]
    shard, _, _, core = place()
    for k in range(tiles):
        for j in range(shards):

            @pl.when((shard ^ j) == owner_ref[k])
            def _(k=k, j=j):
                out_ref[k, :, :LANES], out_ref[k, :, LANES:] = unfold(blocks[j][...], rows, core)


def shape(dims, dtype=F32):
    return jax.ShapeDtypeStruct(dims, dtype)


def kernel_call(body, outs, ins, scratch=(), smem=0, flops=0, mib=16):
    vmem = pl.BlockSpec(memory_space=pltpu.VMEM)
    moved = sum(a.size * a.dtype.itemsize for a in (*ins, *jax.tree.leaves(outs)))
    return pl.pallas_call(
        body,
        out_shape=outs,
        in_specs=[pl.BlockSpec(memory_space=pltpu.SMEM)] * smem + [vmem] * (len(ins) - smem),
        out_specs=jax.tree.map(lambda _: vmem, outs),
        scratch_shapes=list(scratch),
        compiler_params=pltpu.CompilerParams(vmem_limit_bytes=mib << 20),
        cost_estimate=pl.CostEstimate(flops=flops, bytes_accessed=moved, transcendentals=0),
    )(*ins)


def swap(a, axis, mask):
    return lax.ppermute(a, axis, [(i, i ^ mask) for i in range(lax.axis_size(axis))])


def local(
    grad_parts, adam_v, left_stat, right_stat, left_root, right_root, owner, vec_parts, vec_m, vec_v
):
    shards = lax.axis_size("shard")
    tiles, rows, cols = adam_v.shape
    size = grad_parts.shape[3]
    packed = rows + rows // 2

    block = shape((tiles * packed, LANES))
    wide = shape((tiles * packed + EXTRA, LANES))
    sf, sn, kf, kn = kernel_call(
        functools.partial(split_kernel, rows, tiles), (wide, block, wide, block), (grad_parts, vec_parts)
    )
    u = kf + swap(sf, "tensor", 1)
    rn = swap(sn, "tensor", 1)
    r = swap(u, "tensor", 2)
    vec = shape((tiles, rows))
    res = kernel_call(
        functools.partial(adam_kernel, rows, tiles, shards),
        (shape((packed + EXTRA, LANES)),) * shards + (shape(adam_v.shape), vec, vec, vec),
        (owner, kn, rn, u[tiles * packed :], r, adam_v, vec_m, vec_v),
        (pltpu.VMEM((tiles, packed, LANES), F32), pltpu.VMEM((tiles, EXTRA, LANES), F32)),
        smem=1,
    )
    outgoing, (new_adam_v, new_vec_m, new_vec_v, vec_step) = res[:shards], res[shards:]

    roots = jnp.concatenate([left_root, right_root], axis=0)
    roots, outgoing = lax.optimization_barrier((roots, outgoing))
    arrived = [outgoing[0]] + [swap(outgoing[j], "shard", j) for j in range(1, shards)]
    roots_chip, roots_core = swap(roots, "tensor", 2), swap(roots, "tensor", 1)
    full = shape((size, size), BF16)
    left_full, right_full = kernel_call(
        roots_kernel, (full, full), (roots, roots_core, roots_chip, swap(roots_chip, "tensor", 1))
    )
    pieces = []
    for part in (arrived[: shards // 2], arrived[shards // 2 :]):
        mine = jnp.concatenate(part, axis=0)
        across = swap(mine, "tensor", 2)
        pieces += [mine, swap(mine, "tensor", 1), across, swap(across, "tensor", 1)]
    res = kernel_call(
        functools.partial(owner_kernel, rows, shards),
        (shape((packed, LANES)),) * shards + (full, full),
        (*pieces, left_full, right_full),
        (pltpu.VMEM((size, size), BF16), pltpu.VMEM((size, size), BF16), pltpu.VMEM((size, size), F32)),
        flops=8 * size**3,
        mib=32,
    )
    ready, (high, low) = res[:shards], res[shards:]
    back = [ready[0]] + [swap(ready[j], "shard", j) for j in range(1, shards)]
    new_left, new_right = kernel_call(
        functools.partial(stats_kernel, tiles),
        (shape(left_stat.shape), shape(right_stat.shape)),
        (owner, high, low, left_stat, right_stat),
        smem=1,
        flops=12 * cols * size**2,
        mib=32,
    )
    update = kernel_call(
        functools.partial(back_kernel, rows, tiles, shards), shape(adam_v.shape), (owner, *back), smem=1
    )
    return (update, new_adam_v, new_left, new_right, new_vec_m, new_vec_v, vec_step)


def solution(mesh):
    in_specs = (
        P("tensor", None, "shard", None),
        P(None, "shard", "tensor"),
        P("shard", "tensor", None),
        P("shard", "tensor", None),
        P("shard", "tensor", None),
        P("shard", "tensor", None),
        P(),
        P("tensor", None, "shard"),
        P(None, "shard"),
        P(None, "shard"),
    )
    out_specs = (
        P(None, "shard", "tensor"),
        P(None, "shard", "tensor"),
        P("shard", "tensor", None),
        P("shard", "tensor", None),
        P(None, "shard"),
        P(None, "shard"),
        P(None, "shard"),
    )
    packs = mesh.shape["tensor"] == 4 and mesh.shape["shard"] == 8
    return jax.shard_map(
        local if packs else plain, mesh=mesh, in_specs=in_specs, out_specs=out_specs, check_vma=False
    )
```

```python
import functools

import jax
import jax.numpy as jnp
from jax import lax
from jax.experimental import pallas as pl
from jax.experimental.pallas import tpu as pltpu
from jax.sharding import PartitionSpec as P

BETA_ONE = 0.9
BETA_TWO = 0.95
STAT_DECAY = 0.95
STEP_COUNT = 10.0
EPSILON = 1e-08
NORM_EPS = 1e-06
BIAS_ONE = 1.0 - BETA_ONE**STEP_COUNT
BIAS_TWO = 1.0 - BETA_TWO**STEP_COUNT
HIGH = lax.Precision.HIGHEST
LANES = 128
BACK = (1, 2, 4, 5, 6, 7, 3, 0)
EXTRA = 8
F32 = jnp.float32
BF16 = jnp.bfloat16


def plain(
    grad_parts, adam_v, left_stat, right_stat, left_root, right_root, owner, vec_parts, vec_m, vec_v
):
    shards = lax.axis_size("shard")
    tiles = owner.shape[0]
    grad = lax.psum_scatter(grad_parts[0], "tensor", scatter_dimension=2, tiled=True)
    rows_dev = grad.shape[1]
    cols_dev = grad.shape[2]
    new_adam_v = BETA_TWO * adam_v + (1.0 - BETA_TWO) * grad * grad
    adam_dir = grad / (jnp.sqrt(new_adam_v / BIAS_TWO) + EPSILON)
    adam_sq = jnp.sum(adam_dir * adam_dir, axis=(1, 2))
    vec_grad = lax.psum(vec_parts[0], "tensor")
    new_vec_m, new_vec_v, vec_step = vec_update(vec_grad, vec_m, vec_v)
    slot_hot = (jnp.arange(shards, dtype=jnp.int32)[:, None] == owner[None, :]).astype(F32)
    outgoing = jnp.dot(slot_hot, grad.reshape(tiles, rows_dev * cols_dev), precision=HIGH)
    outgoing = outgoing.reshape(shards, rows_dev, cols_dev)
    arrived = lax.all_to_all(outgoing, "shard", split_axis=0, concat_axis=1, tiled=True)[0]
    whole = lax.all_gather(arrived, "tensor", axis=1, tiled=True)
    start = lax.axis_index("tensor") * cols_dev
    tile_rows = lax.dynamic_slice_in_dim(whole, start, cols_dev, 0)
    new_left = STAT_DECAY * left_stat[0] + (1.0 - STAT_DECAY) * jnp.dot(
        tile_rows, whole.T, precision=HIGH
    )
    new_right = STAT_DECAY * right_stat[0] + (1.0 - STAT_DECAY) * jnp.dot(
        arrived.T, whole, precision=HIGH
    )
    left_full = lax.all_gather(left_root[0], "tensor", axis=0, tiled=True).astype(F32)
    right_part = jnp.dot(whole, right_root[0].astype(F32).T, precision=HIGH)
    direction = jnp.dot(left_full, right_part, precision=HIGH)
    returned = lax.all_to_all(
        direction.reshape(shards, rows_dev, cols_dev),
        "shard",
        split_axis=0,
        concat_axis=0,
        tiled=True,
    )
    update = jnp.dot(slot_hot.T, returned.reshape(shards, rows_dev * cols_dev), precision=HIGH)
    update = update.reshape(tiles, rows_dev, cols_dev)
    shampoo_local = jnp.sum(update * update, axis=(1, 2))
    adam_total, shampoo_total = lax.psum((adam_sq, shampoo_local), ("shard", "tensor"))
    graft = jnp.sqrt(adam_total) / (jnp.sqrt(shampoo_total) + NORM_EPS)
    update = graft[:, None, None] * update
    return (update, new_adam_v, new_left[None], new_right[None], new_vec_m, new_vec_v, vec_step)


def vec_update(vec_grad, vec_m, vec_v):
    new_vec_m = BETA_ONE * vec_m + (1.0 - BETA_ONE) * vec_grad
    new_vec_v = BETA_TWO * vec_v + (1.0 - BETA_TWO) * vec_grad * vec_grad
    vec_step = new_vec_m / BIAS_ONE / (jnp.sqrt(new_vec_v / BIAS_TWO) + EPSILON)
    return new_vec_m, new_vec_v, vec_step


def place():
    t = lax.axis_index("tensor")
    return lax.axis_index("shard"), t, t // 2, lax.rem(t, 2)


def lane_tile(index):
    return pl.ds(pl.multiple_of(index * LANES, LANES), LANES)


def swap_halves(a):
    return pltpu.roll(a, LANES // 2, 1)


def low_lanes(rows):
    return lax.broadcasted_iota(jnp.int32, (rows, LANES), 1) < LANES // 2


def fold(mid, core):
    half = mid.shape[0] // 2
    turned = swap_halves(mid)
    first = core == 0
    low = low_lanes(half)
    top = jnp.where(first, mid[:half], turned[:half])
    bottom = jnp.where(first, turned[half:], mid[half:])
    return jnp.where(low, top, bottom)


def unfold(block, rows, core):
    main, side = block[:rows], block[rows:]
    wide = jnp.concatenate([side, swap_halves(side)], axis=0)
    turned = swap_halves(main)
    first = core == 0
    head = jnp.where(first, main, jnp.where(low_lanes(rows), wide, turned))
    return head, jnp.where(first, wide, turned)[:, : LANES // 2]


def split_kernel(rows, tiles, g_ref, vec_ref, sf_ref, sn_ref, kf_ref, kn_ref):
    _, _, chip, core = place()
    packed = rows + rows // 2
    for out, far, own in ((sf_ref, True, False), (sn_ref, False, False), (kf_ref, True, True), (kn_ref, False, True)):
        x = 1 - chip if far else chip
        d = core if own else 1 - core
        for k in range(tiles):
            base = k * packed
            out[base : base + rows] = g_ref[0, k, :, lane_tile(3 * x + 2 * d)]
            out[base + rows : base + packed] = fold(g_ref[0, k, :, lane_tile(3 * x + 1)], d)
        if far:
            out[tiles * packed :] = jnp.zeros((EXTRA, LANES), F32)
            out[tiles * packed : tiles * packed + tiles, : rows] = vec_ref[0]


def tile_of(owner_ref, slot, tiles):
    k = jnp.int32(0)
    for i in range(1, tiles):
        k = jnp.where(owner_ref[i] == slot, i, k)
    return k


def adam_kernel(
    rows, tiles, shards, owner_ref, kn_ref, rn_ref, u_ref, r_ref, v_ref, m_ref, vv_ref, *refs
):
    outs, (nv_ref, vm_ref, vn_ref, vs_ref), (g_ref, ext_ref) = refs[:shards], refs[shards : shards + 4], refs[shards + 4 :]
    shard, _, _, core = place()
    packed = rows + rows // 2

    def one(g, v_old):
        v_new = BETA_TWO * v_old + (1.0 - BETA_TWO) * g * g
        step = g / (jnp.sqrt(v_new / BIAS_TWO) + EPSILON)
        sq = step * step
        return v_new, jnp.sum(sq.reshape(-1, 8, sq.shape[1]), axis=0)

    for k in range(tiles):
        at = slice(k * packed, k * packed + packed)
        g = kn_ref[at] + rn_ref[at] + r_ref[at]
        g_ref[k] = g
        head, tail = unfold(g, rows, core)
        nv_ref[k, :, :LANES], ext_ref[k] = one(head, v_ref[k, :, :LANES])
        nv_ref[k, :, LANES:], sq = one(tail, v_ref[k, :, LANES:])
        ext_ref[k, :, : LANES // 2] += sq
    for j in range(shards):
        k = tile_of(owner_ref, shard ^ j, tiles)
        outs[j][:packed] = g_ref[k]
        outs[j][packed:] = ext_ref[k]
    vec = u_ref[:tiles, :rows] + r_ref[tiles * packed : tiles * packed + tiles, :rows]
    vm_ref[...], vn_ref[...], vs_ref[...] = vec_update(vec, m_ref[...], vv_ref[...])


def roots_kernel(own_ref, core_ref, chip_ref, both_ref, left_ref, right_ref):
    _, t, chip, _ = place()
    rows, size = own_ref.shape[1], left_ref.shape[0]
    half = size // 2
    here = pl.ds(pl.multiple_of(chip * half, half), half)
    there = pl.ds(pl.multiple_of((1 - chip) * half, half), half)

    def block(mask):
        return pl.ds(pl.multiple_of((t ^ mask) * rows, rows), rows)

    for n, ref in enumerate((left_ref, right_ref)):
        ref[block(0), :] = own_ref[n]
        ref[block(1), :] = core_ref[n]
        ref[block(2), there] = chip_ref[n]
        ref[block(3), there] = both_ref[n]
        ref[there, here] = ref[here, there].T


def halves(a):
    high = a.astype(BF16)
    return high, (a - high.astype(F32)).astype(BF16)


def laid_out(mine, peer, i, rows, core):
    packed = rows + rows // 2
    base = i * (packed + EXTRA)
    a, b = mine[base : base + packed], peer[base : base + packed]
    extra = mine[base + packed : base + packed + EXTRA] + peer[base + packed : base + packed + EXTRA]
    first, last = jnp.where(core == 0, a, b), jnp.where(core == 0, b, a)
    fs, ls = first[rows:], last[rows:]
    low = low_lanes(rows // 2)
    mid = jnp.concatenate([jnp.where(low, fs, swap_halves(ls)), jnp.where(low, swap_halves(fs), ls)], axis=0)
    return (first[:rows], mid, last[:rows]), extra


def product(a, b):
    return jnp.dot(a, b, preferred_element_type=F32)


def near_kernel(
    rows, shards, mine_ref, peer_ref, chip_ref, both_ref, far_ref, far_peer_ref, left_ref, right_ref,
    ah_ref, al_ref, bh_ref, bl_ref, z_ref, dir_ref, adam_ref, zh_ref, zl_ref
):
    shard, _, chip, core = place()
    group = shards // 2
    half = group * rows
    adam = jnp.zeros((EXTRA, LANES), F32)
    for i in range(group):
        to = pl.ds(pl.multiple_of((lax.rem(shard, group) ^ i) * rows, rows), rows)
        for x, mine, peer in ((chip, mine_ref, peer_ref), (1 - chip, chip_ref, both_ref)):
            parts, extra = laid_out(mine, peer, i, rows, core)
            adam += extra
            for n, tile in enumerate(parts):
                ah_ref[to, lane_tile(3 * x + n)], al_ref[to, lane_tile(3 * x + n)] = halves(tile)
        parts, extra = laid_out(far_ref, far_peer_ref, i, rows, core)
        adam += extra
        for n, tile in enumerate(parts):
            bh_ref[to, n * LANES : (n + 1) * LANES], bl_ref[to, n * LANES : (n + 1) * LANES] = halves(tile)
    adam_ref[...] = adam
    z = product(ah_ref[...], right_ref[...]) + product(al_ref[...], right_ref[...])
    zh_ref[...], zl_ref[...] = halves(z)
    here = pl.ds(pl.multiple_of(chip * half, half), half)
    z_ref[...] = product(bh_ref[...], right_ref[here, :]) + product(bl_ref[...], right_ref[here, :])
    near = pl.ds(pl.multiple_of(shard // group * half, half), half)
    for n in range(2):
        at = slice(n * half, (n + 1) * half)
        dir_ref[at] = product(left_ref[at, near], zh_ref[...]) + product(left_ref[at, near], zl_ref[...])


def owner_kernel(rows, shards, chip_ref, both_ref, z_ref, part_ref, adam_ref, left_ref, right_ref, *refs):
    (bh_ref, bl_ref), outs, (zh_ref, zl_ref, dir_ref) = refs[:2], refs[2 : shards + 2], refs[shards + 2 :]
    shard, _, chip, core = place()
    group = shards // 2
    half = group * rows
    adam = adam_ref[...]
    for i in range(group):
        to = pl.ds(pl.multiple_of((lax.rem(shard, group) ^ i) * rows, rows), rows)
        parts, extra = laid_out(chip_ref, both_ref, i, rows, core)
        adam += extra
        for n, tile in enumerate(parts):
            bh_ref[to, n * LANES : (n + 1) * LANES], bl_ref[to, n * LANES : (n + 1) * LANES] = halves(tile)
    there = pl.ds(pl.multiple_of((1 - chip) * half, half), half)
    z = z_ref[...] + product(bh_ref[...], right_ref[there, :]) + product(bl_ref[...], right_ref[there, :])
    zh_ref[...], zl_ref[...] = halves(z)
    far = pl.ds(pl.multiple_of((1 - shard // group) * half, half), half)
    squares = jnp.zeros((8, 2 * half), F32)
    for n in range(2):
        at = slice(n * half, (n + 1) * half)
        d = part_ref[at] + product(left_ref[at, far], zh_ref[...]) + product(left_ref[at, far], zl_ref[...])
        dir_ref[at] = d
        squares += jnp.sum((d * d).reshape(-1, 8, 2 * half), axis=0)

    def whole(a):
        return jnp.sum(jnp.sum(a, axis=1, keepdims=True), axis=0, keepdims=True)

    graft = jnp.sqrt(whole(adam)) / (jnp.sqrt(whole(squares)) + NORM_EPS)
    for j, out in zip(BACK, outs):
        at = pl.ds(pl.multiple_of((shard ^ j) * rows, rows), rows)
        out[:rows] = graft * dir_ref[at, lane_tile(3 * chip + 2 * core)]
        out[rows:] = graft * fold(dir_ref[at, lane_tile(3 * chip + 1)], core)


def stats_kernel(tiles, shards, owner_ref, ah_ref, al_ref, bh_ref, bl_ref, ch_ref, cl_ref, left_ref, right_ref, nl_ref, nr_ref, gh_ref, gl_ref):
    shard, t, chip, core = place()
    rows = left_ref.shape[1]
    half = ah_ref.shape[0]
    side = shard // (shards // 2)

    def part(index):
        return pl.ds(pl.multiple_of(index * half, half), half)

    for ref, a, b, c in ((gh_ref, ah_ref, bh_ref, ch_ref), (gl_ref, al_ref, bl_ref, cl_ref)):
        ref[part(side), :] = a[...]
        ref[part(1 - side), part(chip)] = b[...]
        ref[part(1 - side), part(1 - chip)] = c[...]
    held = owner_ref[0] == shard
    for i in range(1, tiles):
        held = jnp.logical_or(held, owner_ref[i] == shard)

    def three(high, low, dims):
        dot = functools.partial(lax.dot_general, dimension_numbers=(dims, ((), ())), preferred_element_type=F32)
        return dot(high, gh_ref[...]) + dot(high, gl_ref[...]) + dot(low, gh_ref[...])

    def refreshed(old, new):
        return STAT_DECAY * old + (1.0 - STAT_DECAY) * jnp.where(held, new, 0.0)

    at = pl.ds(pl.multiple_of(t * rows, rows), rows)
    nl_ref[0] = refreshed(left_ref[0], three(gh_ref[at, :], gl_ref[at, :], ((1,), (1,))))
    end, mid = lane_tile(3 * chip + 2 * core), lane_tile(3 * chip + 1)
    ends = three(gh_ref[:, end], gl_ref[:, end], ((0,), (0,)))
    mids = three(gh_ref[:, mid], gl_ref[:, mid], ((0,), (0,)))
    half = LANES // 2

    @pl.when(core == 0)
    def _():
        nr_ref[0, :LANES] = refreshed(right_ref[0, :LANES], ends)
        nr_ref[0, LANES:] = refreshed(right_ref[0, LANES:], mids[:half])

    @pl.when(core == 1)
    def _():
        nr_ref[0, :half] = refreshed(right_ref[0, :half], mids[half:])
        nr_ref[0, half:] = refreshed(right_ref[0, half:], ends)


def back_kernel(rows, tiles, shards, owner_ref, *refs):
    blocks, out_ref = refs[:shards], refs[shards]
    shard, _, _, core = place()
    for k in range(tiles):
        for j, block in zip(BACK, blocks):

            @pl.when((shard ^ j) == owner_ref[k])
            def _(k=k, block=block):
                out_ref[k, :, :LANES], out_ref[k, :, LANES:] = unfold(block[...], rows, core)


def shape(dims, dtype=F32):
    return jax.ShapeDtypeStruct(dims, dtype)


def kernel_call(body, outs, ins, scratch=(), smem=0, flops=0, mib=16):
    vmem = pl.BlockSpec(memory_space=pltpu.VMEM)
    moved = sum(a.size * a.dtype.itemsize for a in (*ins, *jax.tree.leaves(outs)))
    return pl.pallas_call(
        body,
        out_shape=outs,
        in_specs=[pl.BlockSpec(memory_space=pltpu.SMEM)] * smem + [vmem] * (len(ins) - smem),
        out_specs=jax.tree.map(lambda _: vmem, outs),
        scratch_shapes=list(scratch),
        compiler_params=pltpu.CompilerParams(vmem_limit_bytes=mib << 20),
        cost_estimate=pl.CostEstimate(flops=flops, bytes_accessed=moved, transcendentals=0),
    )(*ins)


def swap(a, axis, mask):
    return lax.ppermute(a, axis, [(i, i ^ mask) for i in range(lax.axis_size(axis))])


def local(
    grad_parts, adam_v, left_stat, right_stat, left_root, right_root, owner, vec_parts, vec_m, vec_v
):
    shards = lax.axis_size("shard")
    tiles, rows, cols = adam_v.shape
    size = grad_parts.shape[3]
    packed = rows + rows // 2

    block = shape((tiles * packed, LANES))
    wide = shape((tiles * packed + EXTRA, LANES))
    sf, sn, kf, kn = kernel_call(
        functools.partial(split_kernel, rows, tiles), (wide, block, wide, block), (grad_parts, vec_parts)
    )
    u = kf + swap(sf, "tensor", 1)
    rn = swap(sn, "tensor", 1)
    r = swap(u, "tensor", 2)
    roots = jnp.concatenate([left_root, right_root], axis=0)
    quadrant = lax.axis_index("tensor") // 2 * (size // 2)
    crossing = lax.dynamic_slice_in_dim(roots, quadrant, size // 2, 2)
    roots_core = swap(roots, "tensor", 1)
    r, roots, roots_core, crossing = lax.optimization_barrier((r, roots, roots_core, crossing))
    vec = shape((tiles, rows))
    res = kernel_call(
        functools.partial(adam_kernel, rows, tiles, shards),
        (shape((packed + EXTRA, LANES)),) * shards + (shape(adam_v.shape), vec, vec, vec),
        (owner, kn, rn, u[tiles * packed :], r, adam_v, vec_m, vec_v),
        (pltpu.VMEM((tiles, packed, LANES), F32), pltpu.VMEM((tiles, EXTRA, LANES), F32)),
        smem=1,
    )
    outgoing, (new_adam_v, new_vec_m, new_vec_v, vec_step) = res[:shards], res[shards:]

    arrived = [outgoing[0]] + [swap(outgoing[j], "shard", j) for j in range(1, shards)]
    roots_chip = swap(crossing, "tensor", 2)
    full = shape((size, size), BF16)
    left_full, right_full = kernel_call(
        roots_kernel, (full, full), (roots, roots_core, roots_chip, swap(roots_chip, "tensor", 1)), mib=24
    )
    near = jnp.concatenate(arrived[: shards // 2], axis=0)
    far = jnp.concatenate(arrived[shards // 2 :], axis=0)
    near_across = swap(near, "tensor", 2)
    near = near, swap(near, "tensor", 1), near_across, swap(near_across, "tensor", 1)
    far_across = swap(far, "tensor", 2)
    half = size // 2
    tall, square = shape((half, size), BF16), shape((half, half), BF16)
    ah, al, bh, bl, z, part, adam = kernel_call(
        functools.partial(near_kernel, rows, shards),
        (tall, tall, square, square, shape((half, size)), shape((size, size)), shape((EXTRA, LANES))),
        (*near, far, swap(far, "tensor", 1), left_full, right_full),
        (pltpu.VMEM((half, size), BF16),) * 2,
        flops=5 * size**3,
        mib=32,
    )
    far_across, adam = lax.optimization_barrier((far_across, adam))
    ch, cl, *ready = kernel_call(
        functools.partial(owner_kernel, rows, shards),
        (square, square) + (shape((packed, LANES)),) * shards,
        (far_across, swap(far_across, "tensor", 1), z, part, adam, left_full, right_full),
        (pltpu.VMEM((half, size), BF16),) * 2 + (pltpu.VMEM((size, size), F32),),
        flops=3 * size**3,
        mib=32,
    )
    back = [swap(block, "shard", j) if j else block for j, block in zip(BACK, ready)]
    new_left, new_right = kernel_call(
        functools.partial(stats_kernel, tiles, shards),
        (shape(left_stat.shape), shape(right_stat.shape)),
        (owner, ah, al, bh, bl, ch, cl, left_stat, right_stat),
        (pltpu.VMEM((size, size), BF16),) * 2,
        smem=1,
        flops=12 * cols * size**2,
        mib=32,
    )
    update = kernel_call(
        functools.partial(back_kernel, rows, tiles, shards), shape(adam_v.shape), (owner, *back), smem=1
    )
    return (update, new_adam_v, new_left, new_right, new_vec_m, new_vec_v, vec_step)


def solution(mesh):
    in_specs = (
        P("tensor", None, "shard", None),
        P(None, "shard", "tensor"),
        P("shard", "tensor", None),
        P("shard", "tensor", None),
        P("shard", "tensor", None),
        P("shard", "tensor", None),
        P(),
        P("tensor", None, "shard"),
        P(None, "shard"),
        P(None, "shard"),
    )
    out_specs = (
        P(None, "shard", "tensor"),
        P(None, "shard", "tensor"),
        P("shard", "tensor", None),
        P("shard", "tensor", None),
        P(None, "shard"),
        P(None, "shard"),
        P(None, "shard"),
    )
    packs = mesh.shape["tensor"] == 4 and mesh.shape["shard"] == 8
    return jax.shard_map(
        local if packs else plain, mesh=mesh, in_specs=in_specs, out_specs=out_specs, check_vma=False
    )
```

```python
import functools

import jax
import jax.numpy as jnp
from jax import lax
from jax.experimental import pallas as pl
from jax.experimental.pallas import tpu as pltpu
from jax.sharding import PartitionSpec as P

BETA_ONE = 0.9
BETA_TWO = 0.95
STAT_DECAY = 0.95
STEP_COUNT = 10.0
EPSILON = 1e-08
NORM_EPS = 1e-06
BIAS_ONE = 1.0 - BETA_ONE**STEP_COUNT
BIAS_TWO = 1.0 - BETA_TWO**STEP_COUNT
HIGH = lax.Precision.HIGHEST
LANES = 128
BACK = (4, 1, 5, 2, 6, 3, 7, 0)
EXTRA = 8
F32 = jnp.float32
BF16 = jnp.bfloat16


def plain(
    grad_parts, adam_v, left_stat, right_stat, left_root, right_root, owner, vec_parts, vec_m, vec_v
):
    shards = lax.axis_size("shard")
    tiles = owner.shape[0]
    grad = lax.psum_scatter(grad_parts[0], "tensor", scatter_dimension=2, tiled=True)
    rows_dev = grad.shape[1]
    cols_dev = grad.shape[2]
    new_adam_v = BETA_TWO * adam_v + (1.0 - BETA_TWO) * grad * grad
    adam_dir = grad / (jnp.sqrt(new_adam_v / BIAS_TWO) + EPSILON)
    adam_sq = jnp.sum(adam_dir * adam_dir, axis=(1, 2))
    vec_grad = lax.psum(vec_parts[0], "tensor")
    new_vec_m, new_vec_v, vec_step = vec_update(vec_grad, vec_m, vec_v)
    slot_hot = (jnp.arange(shards, dtype=jnp.int32)[:, None] == owner[None, :]).astype(F32)
    outgoing = jnp.dot(slot_hot, grad.reshape(tiles, rows_dev * cols_dev), precision=HIGH)
    outgoing = outgoing.reshape(shards, rows_dev, cols_dev)
    arrived = lax.all_to_all(outgoing, "shard", split_axis=0, concat_axis=1, tiled=True)[0]
    whole = lax.all_gather(arrived, "tensor", axis=1, tiled=True)
    start = lax.axis_index("tensor") * cols_dev
    tile_rows = lax.dynamic_slice_in_dim(whole, start, cols_dev, 0)
    new_left = STAT_DECAY * left_stat[0] + (1.0 - STAT_DECAY) * jnp.dot(
        tile_rows, whole.T, precision=HIGH
    )
    new_right = STAT_DECAY * right_stat[0] + (1.0 - STAT_DECAY) * jnp.dot(
        arrived.T, whole, precision=HIGH
    )
    left_full = lax.all_gather(left_root[0], "tensor", axis=0, tiled=True).astype(F32)
    right_part = jnp.dot(whole, right_root[0].astype(F32).T, precision=HIGH)
    direction = jnp.dot(left_full, right_part, precision=HIGH)
    returned = lax.all_to_all(
        direction.reshape(shards, rows_dev, cols_dev),
        "shard",
        split_axis=0,
        concat_axis=0,
        tiled=True,
    )
    update = jnp.dot(slot_hot.T, returned.reshape(shards, rows_dev * cols_dev), precision=HIGH)
    update = update.reshape(tiles, rows_dev, cols_dev)
    shampoo_local = jnp.sum(update * update, axis=(1, 2))
    adam_total, shampoo_total = lax.psum((adam_sq, shampoo_local), ("shard", "tensor"))
    graft = jnp.sqrt(adam_total) / (jnp.sqrt(shampoo_total) + NORM_EPS)
    update = graft[:, None, None] * update
    return (update, new_adam_v, new_left[None], new_right[None], new_vec_m, new_vec_v, vec_step)


def vec_update(vec_grad, vec_m, vec_v):
    new_vec_m = BETA_ONE * vec_m + (1.0 - BETA_ONE) * vec_grad
    new_vec_v = BETA_TWO * vec_v + (1.0 - BETA_TWO) * vec_grad * vec_grad
    vec_step = new_vec_m / BIAS_ONE / (jnp.sqrt(new_vec_v / BIAS_TWO) + EPSILON)
    return new_vec_m, new_vec_v, vec_step


def place():
    t = lax.axis_index("tensor")
    return lax.axis_index("shard"), t, t // 2, lax.rem(t, 2)


def lane_tile(index):
    return pl.ds(pl.multiple_of(index * LANES, LANES), LANES)


def swap_halves(a):
    return pltpu.roll(a, LANES // 2, 1)


def low_lanes(rows):
    return lax.broadcasted_iota(jnp.int32, (rows, LANES), 1) < LANES // 2


def fold(mid, core):
    half = mid.shape[0] // 2
    turned = swap_halves(mid)
    first = core == 0
    low = low_lanes(half)
    top = jnp.where(first, mid[:half], turned[:half])
    bottom = jnp.where(first, turned[half:], mid[half:])
    return jnp.where(low, top, bottom)


def unfold(block, rows, core):
    main, side = block[:rows], block[rows:]
    wide = jnp.concatenate([side, swap_halves(side)], axis=0)
    turned = swap_halves(main)
    first = core == 0
    head = jnp.where(first, main, jnp.where(low_lanes(rows), wide, turned))
    return head, jnp.where(first, wide, turned)[:, : LANES // 2]


def split_kernel(rows, tiles, far, g_ref, *refs):
    vec_ref, send_ref, keep_ref = refs if len(refs) == 3 else (None, *refs)
    _, _, chip, core = place()
    packed = rows + rows // 2
    x = 1 - chip if far else chip
    for out, d in ((send_ref, 1 - core), (keep_ref, core)):
        for k in range(tiles):
            base = k * packed
            out[base : base + rows] = g_ref[0, k, :, lane_tile(3 * x + 2 * d)]
            out[base + rows : base + packed] = fold(g_ref[0, k, :, lane_tile(3 * x + 1)], d)
        if vec_ref is not None:
            out[tiles * packed :] = jnp.zeros((EXTRA, LANES), F32)
            out[tiles * packed : tiles * packed + tiles, :rows] = vec_ref[0]


def tile_of(owner_ref, slot, tiles):
    k = jnp.int32(0)
    for i in range(1, tiles):
        k = jnp.where(owner_ref[i] == slot, i, k)
    return k


def adam_kernel(
    rows, tiles, shards, owner_ref, kn_ref, rn_ref, r_ref, v_ref, *refs
):
    outs, (nv_ref, vec_ref, g_ref, ext_ref) = refs[:shards], refs[shards:]
    shard, _, _, core = place()
    packed = rows + rows // 2

    def one(g, v_old):
        v_new = BETA_TWO * v_old + (1.0 - BETA_TWO) * g * g
        step = g / (jnp.sqrt(v_new * (1.0 / BIAS_TWO)) + EPSILON)
        sq = step * step
        return v_new, jnp.sum(sq.reshape(-1, 8, sq.shape[1]), axis=0)

    for k in range(tiles):
        at = slice(k * packed, k * packed + packed)
        g = kn_ref[at] + rn_ref[at] + r_ref[at]
        g_ref[k] = g
        head, tail = unfold(g, rows, core)
        nv_ref[k, :, :LANES], ext_ref[k] = one(head, v_ref[k, :, :LANES])
        nv_ref[k, :, LANES:], sq = one(tail, v_ref[k, :, LANES:])
        ext_ref[k, :, : LANES // 2] += sq
    for j in range(shards):
        k = tile_of(owner_ref, shard ^ j, tiles)
        outs[j][:packed] = g_ref[k]
        outs[j][packed:] = ext_ref[k]
    vec_ref[...] = kn_ref[tiles * packed :] + rn_ref[tiles * packed :]


def roots_kernel(own_ref, core_ref, chip_ref, both_ref, left_ref, right_ref):
    _, t, chip, _ = place()
    rows, size = own_ref.shape[1], left_ref.shape[0]
    half = size // 2
    here = pl.ds(pl.multiple_of(chip * half, half), half)
    there = pl.ds(pl.multiple_of((1 - chip) * half, half), half)

    def block(mask):
        return pl.ds(pl.multiple_of((t ^ mask) * rows, rows), rows)

    for n, ref in enumerate((left_ref, right_ref)):
        ref[block(0), :] = own_ref[n]
        ref[block(1), :] = core_ref[n]
        ref[block(2), there] = chip_ref[n]
        ref[block(3), there] = both_ref[n]
        ref[there, here] = ref[here, there].T


def halves(a):
    high = a.astype(BF16)
    return high, (a - high.astype(F32)).astype(BF16)


def laid_out(mine, peer, i, rows, core):
    packed = rows + rows // 2
    base = i * (packed + EXTRA)
    a, b = mine[base : base + packed], peer[base : base + packed]
    extra = mine[base + packed : base + packed + EXTRA] + peer[base + packed : base + packed + EXTRA]
    first, last = jnp.where(core == 0, a, b), jnp.where(core == 0, b, a)
    fs, ls = first[rows:], last[rows:]
    low = low_lanes(rows // 2)
    mid = jnp.concatenate([jnp.where(low, fs, swap_halves(ls)), jnp.where(low, swap_halves(fs), ls)], axis=0)
    return (first[:rows], mid, last[:rows]), extra


def product(a, b):
    return jnp.dot(a, b, preferred_element_type=F32)


def near_kernel(
    rows, shards, mine_ref, peer_ref, chip_ref, both_ref, far_ref, far_peer_ref, left_ref, right_ref,
    m_ref, v_ref, adam_new, ah_ref, al_ref, bh_ref, bl_ref, z_ref, dir_ref, adam_ref, nm_ref, nv_ref, step_ref,
    adam_out, zh_ref, zl_ref
):
    shard, _, chip, core = place()
    group = shards // 2
    half = group * rows
    adam = jnp.zeros((EXTRA, LANES), F32)
    for i in range(group):
        to = pl.ds(pl.multiple_of((lax.rem(shard, group) ^ i) * rows, rows), rows)
        for x, mine, peer in ((chip, mine_ref, peer_ref), (1 - chip, chip_ref, both_ref)):
            parts, extra = laid_out(mine, peer, i, rows, core)
            adam += extra
            for n, tile in enumerate(parts):
                ah_ref[to, lane_tile(3 * x + n)], al_ref[to, lane_tile(3 * x + n)] = halves(tile)
        parts, extra = laid_out(far_ref, far_peer_ref, i, rows, core)
        adam += extra
        for n, tile in enumerate(parts):
            bh_ref[to, n * LANES : (n + 1) * LANES], bl_ref[to, n * LANES : (n + 1) * LANES] = halves(tile)
    adam_ref[...] = adam
    end = group * (rows + rows // 2 + EXTRA)
    vecs, wide = m_ref.shape
    vec = mine_ref[end : end + vecs, :wide] + chip_ref[end : end + vecs, :wide]
    nm_ref[...], nv_ref[...], step_ref[...] = vec_update(vec, m_ref[...], v_ref[...])
    adam_out[...] = adam_new[...]
    z = product(ah_ref[...], right_ref[...]) + product(al_ref[...], right_ref[...])
    zh_ref[...], zl_ref[...] = halves(z)
    here = pl.ds(pl.multiple_of(chip * half, half), half)
    z_ref[...] = product(bh_ref[...], right_ref[here, :]) + product(bl_ref[...], right_ref[here, :])
    near = pl.ds(pl.multiple_of(shard // group * half, half), half)
    for n in range(2):
        at = slice(n * half, (n + 1) * half)
        dir_ref[at] = product(left_ref[at, near], zh_ref[...]) + product(left_ref[at, near], zl_ref[...])


def owner_kernel(rows, shards, chip_ref, both_ref, z_ref, part_ref, adam_ref, left_ref, right_ref, *refs):
    (bh_ref, bl_ref), outs, (zh_ref, zl_ref, dir_ref) = refs[:2], refs[2 : shards + 2], refs[shards + 2 :]
    shard, _, chip, core = place()
    group = shards // 2
    half = group * rows
    adam = adam_ref[...]
    for i in range(group):
        to = pl.ds(pl.multiple_of((lax.rem(shard, group) ^ i) * rows, rows), rows)
        parts, extra = laid_out(chip_ref, both_ref, i, rows, core)
        adam += extra
        for n, tile in enumerate(parts):
            bh_ref[to, n * LANES : (n + 1) * LANES], bl_ref[to, n * LANES : (n + 1) * LANES] = halves(tile)
    there = pl.ds(pl.multiple_of((1 - chip) * half, half), half)
    z = z_ref[...] + product(bh_ref[...], right_ref[there, :]) + product(bl_ref[...], right_ref[there, :])
    zh_ref[...], zl_ref[...] = halves(z)
    far = pl.ds(pl.multiple_of((1 - shard // group) * half, half), half)
    squares = jnp.zeros((8, 2 * half), F32)
    for n in range(2):
        at = slice(n * half, (n + 1) * half)
        d = part_ref[at] + product(left_ref[at, far], zh_ref[...]) + product(left_ref[at, far], zl_ref[...])
        dir_ref[at] = d
        squares += jnp.sum((d * d).reshape(-1, 8, 2 * half), axis=0)

    def whole(a):
        return jnp.sum(jnp.sum(a, axis=1, keepdims=True), axis=0, keepdims=True)

    graft = jnp.sqrt(whole(adam)) / (jnp.sqrt(whole(squares)) + NORM_EPS)
    for j, out in zip(BACK, outs):
        at = pl.ds(pl.multiple_of((shard ^ j) * rows, rows), rows)
        out[:rows] = graft * dir_ref[at, lane_tile(3 * chip + 2 * core)]
        out[rows:] = graft * fold(dir_ref[at, lane_tile(3 * chip + 1)], core)


def stats_kernel(tiles, shards, owner_ref, ah_ref, al_ref, bh_ref, bl_ref, ch_ref, cl_ref, left_ref, right_ref, nl_ref, nr_ref, gh_ref, gl_ref):
    shard, t, chip, core = place()
    rows = left_ref.shape[1]
    half = ah_ref.shape[0]
    side = shard // (shards // 2)

    def part(index):
        return pl.ds(pl.multiple_of(index * half, half), half)

    for ref, a, b, c in ((gh_ref, ah_ref, bh_ref, ch_ref), (gl_ref, al_ref, bl_ref, cl_ref)):
        ref[part(side), :] = a[...]
        ref[part(1 - side), part(chip)] = b[...]
        ref[part(1 - side), part(1 - chip)] = c[...]
    held = owner_ref[0] == shard
    for i in range(1, tiles):
        held = jnp.logical_or(held, owner_ref[i] == shard)

    def three(high, low, dims):
        dot = functools.partial(lax.dot_general, dimension_numbers=(dims, ((), ())), preferred_element_type=F32)
        return dot(high, gh_ref[...]) + dot(high, gl_ref[...]) + dot(low, gh_ref[...])

    def refreshed(old, new):
        return STAT_DECAY * old + (1.0 - STAT_DECAY) * jnp.where(held, new, 0.0)

    at = pl.ds(pl.multiple_of(t * rows, rows), rows)
    nl_ref[0] = refreshed(left_ref[0], three(gh_ref[at, :], gl_ref[at, :], ((1,), (1,))))
    end, mid = lane_tile(3 * chip + 2 * core), lane_tile(3 * chip + 1)
    ends = three(gh_ref[:, end], gl_ref[:, end], ((0,), (0,)))
    mids = three(gh_ref[:, mid], gl_ref[:, mid], ((0,), (0,)))
    half = LANES // 2

    @pl.when(core == 0)
    def _():
        nr_ref[0, :LANES] = refreshed(right_ref[0, :LANES], ends)
        nr_ref[0, LANES:] = refreshed(right_ref[0, LANES:], mids[:half])

    @pl.when(core == 1)
    def _():
        nr_ref[0, :half] = refreshed(right_ref[0, :half], mids[half:])
        nr_ref[0, half:] = refreshed(right_ref[0, half:], ends)


def back_kernel(rows, tiles, shards, owner_ref, *refs):
    blocks, out_ref = refs[:shards], refs[shards]
    shard, _, _, core = place()
    for j, block in zip(BACK, blocks):
        k = tile_of(owner_ref, shard ^ j, tiles)

        @pl.when(owner_ref[k] == (shard ^ j))
        def _(k=k, block=block):
            out_ref[k, :, :LANES], out_ref[k, :, LANES:] = unfold(block[...], rows, core)


def shape(dims, dtype=F32):
    return jax.ShapeDtypeStruct(dims, dtype)


def kernel_call(body, outs, ins, scratch=(), smem=0, flops=0, mib=16):
    vmem = pl.BlockSpec(memory_space=pltpu.VMEM)
    moved = sum(a.size * a.dtype.itemsize for a in (*ins, *jax.tree.leaves(outs)))
    return pl.pallas_call(
        body,
        out_shape=outs,
        in_specs=[pl.BlockSpec(memory_space=pltpu.SMEM)] * smem + [vmem] * (len(ins) - smem),
        out_specs=jax.tree.map(lambda _: vmem, outs),
        scratch_shapes=list(scratch),
        compiler_params=pltpu.CompilerParams(vmem_limit_bytes=mib << 20),
        cost_estimate=pl.CostEstimate(flops=flops, bytes_accessed=moved, transcendentals=0),
    )(*ins)


def swap(a, axis, mask):
    return lax.ppermute(a, axis, [(i, i ^ mask) for i in range(lax.axis_size(axis))])


def local(
    grad_parts, adam_v, left_stat, right_stat, left_root, right_root, owner, vec_parts, vec_m, vec_v
):
    shards = lax.axis_size("shard")
    tiles, rows, cols = adam_v.shape
    size = grad_parts.shape[3]
    packed = rows + rows // 2

    block = shape((tiles * packed, LANES))
    wide = shape((tiles * packed + EXTRA, LANES))
    sf, kf = kernel_call(functools.partial(split_kernel, rows, tiles, True), (block, block), (grad_parts,))
    sn, kn = kernel_call(functools.partial(split_kernel, rows, tiles, False), (wide, wide), (grad_parts, vec_parts))
    u = kf + swap(sf, "tensor", 1)
    rn = swap(sn, "tensor", 1)
    r = swap(u, "tensor", 2)
    roots = jnp.concatenate([left_root, right_root], axis=0)
    quadrant = lax.axis_index("tensor") // 2 * (size // 2)
    crossing = lax.dynamic_slice_in_dim(roots, quadrant, size // 2, 2)
    roots_core = swap(roots, "tensor", 1)
    r, roots, roots_core, crossing = lax.optimization_barrier((r, roots, roots_core, crossing))
    res = kernel_call(
        functools.partial(adam_kernel, rows, tiles, shards),
        (shape((packed + EXTRA, LANES)),) * shards + (shape(adam_v.shape), shape((EXTRA, LANES))),
        (owner, kn, rn, r, adam_v),
        (pltpu.VMEM((tiles, packed, LANES), F32), pltpu.VMEM((tiles, EXTRA, LANES), F32)),
        smem=1,
    )
    outgoing, (adam_new, vec_pair) = res[:shards], res[shards:]

    arrived = [outgoing[0]] + [swap(outgoing[j], "shard", j) for j in range(1, shards)]
    roots_chip = swap(crossing, "tensor", 2)
    full = shape((size, size), BF16)
    left_full, right_full = kernel_call(
        roots_kernel, (full, full), (roots, roots_core, roots_chip, swap(roots_chip, "tensor", 1)), mib=24
    )
    near = jnp.concatenate([*arrived[: shards // 2], vec_pair], axis=0)
    far = jnp.concatenate(arrived[shards // 2 :], axis=0)
    near_across = swap(near, "tensor", 2)
    near = near, swap(near, "tensor", 1), near_across, swap(near_across, "tensor", 1)
    far_across = swap(far, "tensor", 2)
    half = size // 2
    tall, square = shape((half, size), BF16), shape((half, half), BF16)
    vec = shape(vec_m.shape)
    ah, al, bh, bl, z, part, adam, new_vec_m, new_vec_v, vec_step, new_adam_v = kernel_call(
        functools.partial(near_kernel, rows, shards),
        (tall, tall, square, square, shape((half, size)), shape((size, size)), shape((EXTRA, LANES)), vec, vec, vec, shape(adam_v.shape)),
        (*near, far, swap(far, "tensor", 1), left_full, right_full, vec_m, vec_v, adam_new),
        (pltpu.VMEM((half, size), BF16),) * 2,
        flops=5 * size**3,
        mib=32,
    )
    far_across, adam = lax.optimization_barrier((far_across, adam))
    ch, cl, *ready = kernel_call(
        functools.partial(owner_kernel, rows, shards),
        (square, square) + (shape((packed, LANES)),) * shards,
        (far_across, swap(far_across, "tensor", 1), z, part, adam, left_full, right_full),
        (pltpu.VMEM((half, size), BF16),) * 2 + (pltpu.VMEM((size, size), F32),),
        flops=3 * size**3,
        mib=32,
    )
    back = [swap(block, "shard", j) if j else block for j, block in zip(BACK, ready)]
    new_left, new_right = kernel_call(
        functools.partial(stats_kernel, tiles, shards),
        (shape(left_stat.shape), shape(right_stat.shape)),
        (owner, ah, al, bh, bl, ch, cl, left_stat, right_stat),
        (pltpu.VMEM((size, size), BF16),) * 2,
        smem=1,
        flops=12 * cols * size**2,
        mib=32,
    )
    update = kernel_call(
        functools.partial(back_kernel, rows, tiles, shards), shape(adam_v.shape), (owner, *back), smem=1
    )
    return (update, new_adam_v, new_left, new_right, new_vec_m, new_vec_v, vec_step)


def solution(mesh):
    in_specs = (
        P("tensor", None, "shard", None),
        P(None, "shard", "tensor"),
        P("shard", "tensor", None),
        P("shard", "tensor", None),
        P("shard", "tensor", None),
        P("shard", "tensor", None),
        P(),
        P("tensor", None, "shard"),
        P(None, "shard"),
        P(None, "shard"),
    )
    out_specs = (
        P(None, "shard", "tensor"),
        P(None, "shard", "tensor"),
        P("shard", "tensor", None),
        P("shard", "tensor", None),
        P(None, "shard"),
        P(None, "shard"),
        P(None, "shard"),
    )
    packs = mesh.shape["tensor"] == 4 and mesh.shape["shard"] == 8
    return jax.shard_map(
        local if packs else plain, mesh=mesh, in_specs=in_specs, out_specs=out_specs, check_vma=False
    )
```

```python
import functools

import jax
import jax.numpy as jnp
from jax import lax
from jax.experimental import pallas as pl
from jax.experimental.pallas import tpu as pltpu
from jax.sharding import PartitionSpec as P

BETA_ONE = 0.9
BETA_TWO = 0.95
STAT_DECAY = 0.95
STEP_COUNT = 10.0
EPSILON = 1e-08
NORM_EPS = 1e-06
BIAS_ONE = 1.0 - BETA_ONE**STEP_COUNT
BIAS_TWO = 1.0 - BETA_TWO**STEP_COUNT
HIGH = lax.Precision.HIGHEST
LANES = 128
BACK = (4, 1, 5, 2, 6, 3, 7, 0)
EXTRA = 8
F32 = jnp.float32
BF16 = jnp.bfloat16


def plain(
    grad_parts, adam_v, left_stat, right_stat, left_root, right_root, owner, vec_parts, vec_m, vec_v
):
    shards = lax.axis_size("shard")
    tiles = owner.shape[0]
    grad = lax.psum_scatter(grad_parts[0], "tensor", scatter_dimension=2, tiled=True)
    rows_dev = grad.shape[1]
    cols_dev = grad.shape[2]
    new_adam_v = BETA_TWO * adam_v + (1.0 - BETA_TWO) * grad * grad
    adam_dir = grad / (jnp.sqrt(new_adam_v / BIAS_TWO) + EPSILON)
    adam_sq = jnp.sum(adam_dir * adam_dir, axis=(1, 2))
    vec_grad = lax.psum(vec_parts[0], "tensor")
    new_vec_m, new_vec_v, vec_step = vec_update(vec_grad, vec_m, vec_v)
    slot_hot = (jnp.arange(shards, dtype=jnp.int32)[:, None] == owner[None, :]).astype(F32)
    outgoing = jnp.dot(slot_hot, grad.reshape(tiles, rows_dev * cols_dev), precision=HIGH)
    outgoing = outgoing.reshape(shards, rows_dev, cols_dev)
    arrived = lax.all_to_all(outgoing, "shard", split_axis=0, concat_axis=1, tiled=True)[0]
    whole = lax.all_gather(arrived, "tensor", axis=1, tiled=True)
    start = lax.axis_index("tensor") * cols_dev
    tile_rows = lax.dynamic_slice_in_dim(whole, start, cols_dev, 0)
    new_left = STAT_DECAY * left_stat[0] + (1.0 - STAT_DECAY) * jnp.dot(
        tile_rows, whole.T, precision=HIGH
    )
    new_right = STAT_DECAY * right_stat[0] + (1.0 - STAT_DECAY) * jnp.dot(
        arrived.T, whole, precision=HIGH
    )
    left_full = lax.all_gather(left_root[0], "tensor", axis=0, tiled=True).astype(F32)
    right_part = jnp.dot(whole, right_root[0].astype(F32).T, precision=HIGH)
    direction = jnp.dot(left_full, right_part, precision=HIGH)
    returned = lax.all_to_all(
        direction.reshape(shards, rows_dev, cols_dev),
        "shard",
        split_axis=0,
        concat_axis=0,
        tiled=True,
    )
    update = jnp.dot(slot_hot.T, returned.reshape(shards, rows_dev * cols_dev), precision=HIGH)
    update = update.reshape(tiles, rows_dev, cols_dev)
    shampoo_local = jnp.sum(update * update, axis=(1, 2))
    adam_total, shampoo_total = lax.psum((adam_sq, shampoo_local), ("shard", "tensor"))
    graft = jnp.sqrt(adam_total) / (jnp.sqrt(shampoo_total) + NORM_EPS)
    update = graft[:, None, None] * update
    return (update, new_adam_v, new_left[None], new_right[None], new_vec_m, new_vec_v, vec_step)


def vec_update(vec_grad, vec_m, vec_v):
    new_vec_m = BETA_ONE * vec_m + (1.0 - BETA_ONE) * vec_grad
    new_vec_v = BETA_TWO * vec_v + (1.0 - BETA_TWO) * vec_grad * vec_grad
    vec_step = new_vec_m / BIAS_ONE / (jnp.sqrt(new_vec_v / BIAS_TWO) + EPSILON)
    return new_vec_m, new_vec_v, vec_step


def place():
    t = lax.axis_index("tensor")
    return lax.axis_index("shard"), t, t // 2, lax.rem(t, 2)


def lane_tile(index):
    return pl.ds(pl.multiple_of(index * LANES, LANES), LANES)


def swap_halves(a):
    return pltpu.roll(a, LANES // 2, 1)


def low_lanes(rows):
    return lax.broadcasted_iota(jnp.int32, (rows, LANES), 1) < LANES // 2


def fold(mid, core):
    half = mid.shape[0] // 2
    turned = swap_halves(mid)
    first = core == 0
    low = low_lanes(half)
    top = jnp.where(first, mid[:half], turned[:half])
    bottom = jnp.where(first, turned[half:], mid[half:])
    return jnp.where(low, top, bottom)


def unfold(block, rows, core):
    main, side = block[:rows], block[rows:]
    wide = jnp.concatenate([side, swap_halves(side)], axis=0)
    turned = swap_halves(main)
    first = core == 0
    head = jnp.where(first, main, jnp.where(low_lanes(rows), wide, turned))
    return head, jnp.where(first, wide, turned)[:, : LANES // 2]


def split_kernel(rows, tiles, far, g_ref, *refs):
    vec_ref, send_ref, keep_ref = refs if len(refs) == 3 else (None, *refs)
    _, _, chip, core = place()
    packed = rows + rows // 2
    x = 1 - chip if far else chip
    for out, d in ((send_ref, 1 - core), (keep_ref, core)):
        for k in range(tiles):
            base = k * packed
            out[base : base + rows] = g_ref[0, k, :, lane_tile(3 * x + 2 * d)]
            out[base + rows : base + packed] = fold(g_ref[0, k, :, lane_tile(3 * x + 1)], d)
        if vec_ref is not None:
            out[tiles * packed :] = jnp.zeros((EXTRA, LANES), F32)
            out[tiles * packed : tiles * packed + tiles, :rows] = vec_ref[0]


def tile_of(owner_ref, slot, tiles):
    k = jnp.int32(0)
    for i in range(1, tiles):
        k = jnp.where(owner_ref[i] == slot, i, k)
    return k


def adam_kernel(
    rows, tiles, shards, owner_ref, kn_ref, rn_ref, r_ref, v_ref, *refs
):
    outs, (nv_ref, vec_ref, g_ref, ext_ref) = refs[:shards], refs[shards:]
    shard, _, _, core = place()
    packed = rows + rows // 2

    def one(g, v_old):
        v_new = BETA_TWO * v_old + (1.0 - BETA_TWO) * g * g
        step = g / (jnp.sqrt(v_new * (1.0 / BIAS_TWO)) + EPSILON)
        sq = step * step
        return v_new, jnp.sum(sq.reshape(-1, 8, sq.shape[1]), axis=0)

    for k in range(tiles):
        at = slice(k * packed, k * packed + packed)
        g = kn_ref[at] + rn_ref[at] + r_ref[at]
        g_ref[k] = g
        head, tail = unfold(g, rows, core)
        nv_ref[k, :, :LANES], ext_ref[k] = one(head, v_ref[k, :, :LANES])
        nv_ref[k, :, LANES:], sq = one(tail, v_ref[k, :, LANES:])
        ext_ref[k, :, : LANES // 2] += sq
    for j in range(shards):
        k = tile_of(owner_ref, shard ^ j, tiles)
        outs[j][:packed] = g_ref[k]
        outs[j][packed:] = ext_ref[k]
    vec_ref[...] = kn_ref[tiles * packed :] + rn_ref[tiles * packed :]


def roots_kernel(own_ref, core_ref, chip_ref, both_ref, left_ref, right_ref):
    _, t, chip, _ = place()
    rows, size = own_ref.shape[1], left_ref.shape[0]
    half = size // 2
    here = pl.ds(pl.multiple_of(chip * half, half), half)
    there = pl.ds(pl.multiple_of((1 - chip) * half, half), half)

    def block(mask):
        return pl.ds(pl.multiple_of((t ^ mask) * rows, rows), rows)

    for n, ref in enumerate((left_ref, right_ref)):
        ref[block(0), :] = own_ref[n]
        ref[block(1), :] = core_ref[n]
        ref[block(2), there] = chip_ref[n]
        ref[block(3), there] = both_ref[n]
        ref[there, here] = ref[here, there].T


def halves(a):
    high = a.astype(BF16)
    return high, (a - high.astype(F32)).astype(BF16)


def laid_out(mine, peer, i, rows, core):
    packed = rows + rows // 2
    base = i * (packed + EXTRA)
    a, b = mine[base : base + packed], peer[base : base + packed]
    extra = mine[base + packed : base + packed + EXTRA] + peer[base + packed : base + packed + EXTRA]
    first, last = jnp.where(core == 0, a, b), jnp.where(core == 0, b, a)
    fs, ls = first[rows:], last[rows:]
    low = low_lanes(rows // 2)
    mid = jnp.concatenate([jnp.where(low, fs, swap_halves(ls)), jnp.where(low, swap_halves(fs), ls)], axis=0)
    return (first[:rows], mid, last[:rows]), extra


def product(a, b):
    return jnp.dot(a, b, preferred_element_type=F32)


def near_kernel(
    rows, shards, mine_ref, peer_ref, chip_ref, both_ref, far_ref, far_peer_ref, left_ref, right_ref,
    m_ref, v_ref, adam_new, ah_ref, al_ref, bh_ref, bl_ref, z_ref, dir_ref, adam_ref, nm_ref, nv_ref, step_ref,
    adam_out, zh_ref, zl_ref
):
    shard, _, chip, core = place()
    group = shards // 2
    half = group * rows
    adam = jnp.zeros((EXTRA, LANES), F32)
    for i in range(group):
        to = pl.ds(pl.multiple_of((lax.rem(shard, group) ^ i) * rows, rows), rows)
        for x, mine, peer in ((chip, mine_ref, peer_ref), (1 - chip, chip_ref, both_ref)):
            parts, extra = laid_out(mine, peer, i, rows, core)
            adam += extra
            for n, tile in enumerate(parts):
                ah_ref[to, lane_tile(3 * x + n)], al_ref[to, lane_tile(3 * x + n)] = halves(tile)
        parts, extra = laid_out(far_ref, far_peer_ref, i, rows, core)
        adam += extra
        for n, tile in enumerate(parts):
            bh_ref[to, n * LANES : (n + 1) * LANES], bl_ref[to, n * LANES : (n + 1) * LANES] = halves(tile)
    adam_ref[...] = adam
    end = group * (rows + rows // 2 + EXTRA)
    vecs, wide = m_ref.shape
    vec = mine_ref[end : end + vecs, :wide] + chip_ref[end : end + vecs, :wide]
    nm_ref[...], nv_ref[...], step_ref[...] = vec_update(vec, m_ref[...], v_ref[...])
    adam_out[...] = adam_new[...]
    z = product(ah_ref[...], right_ref[...]) + product(al_ref[...], right_ref[...])
    zh_ref[...], zl_ref[...] = halves(z)
    here = pl.ds(pl.multiple_of(chip * half, half), half)
    z_ref[...] = product(bh_ref[...], right_ref[here, :]) + product(bl_ref[...], right_ref[here, :])
    near = pl.ds(pl.multiple_of(shard // group * half, half), half)
    for n in range(2):
        at = slice(n * half, (n + 1) * half)
        dir_ref[at] = product(left_ref[at, near], zh_ref[...]) + product(left_ref[at, near], zl_ref[...])


def owner_kernel(rows, shards, chip_ref, both_ref, z_ref, part_ref, adam_ref, left_ref, right_ref, *refs):
    (bh_ref, bl_ref), outs, (zh_ref, zl_ref, dir_ref) = refs[:2], refs[2 : shards + 2], refs[shards + 2 :]
    shard, _, chip, core = place()
    group = shards // 2
    half = group * rows
    adam = adam_ref[...]
    for i in range(group):
        to = pl.ds(pl.multiple_of((lax.rem(shard, group) ^ i) * rows, rows), rows)
        parts, extra = laid_out(chip_ref, both_ref, i, rows, core)
        adam += extra
        for n, tile in enumerate(parts):
            bh_ref[to, n * LANES : (n + 1) * LANES], bl_ref[to, n * LANES : (n + 1) * LANES] = halves(tile)
    there = pl.ds(pl.multiple_of((1 - chip) * half, half), half)
    z = z_ref[...] + product(bh_ref[...], right_ref[there, :]) + product(bl_ref[...], right_ref[there, :])
    zh_ref[...], zl_ref[...] = halves(z)
    far = pl.ds(pl.multiple_of((1 - shard // group) * half, half), half)
    squares = jnp.zeros((8, 2 * half), F32)
    for n in range(2):
        at = slice(n * half, (n + 1) * half)
        d = part_ref[at] + product(left_ref[at, far], zh_ref[...]) + product(left_ref[at, far], zl_ref[...])
        dir_ref[at] = d
        squares += jnp.sum((d * d).reshape(-1, 8, 2 * half), axis=0)

    def whole(a):
        return jnp.sum(jnp.sum(a, axis=1, keepdims=True), axis=0, keepdims=True)

    graft = jnp.sqrt(whole(adam)) / (jnp.sqrt(whole(squares)) + NORM_EPS)
    for j, out in zip(BACK, outs):
        at = pl.ds(pl.multiple_of((shard ^ j) * rows, rows), rows)
        out[:rows] = graft * dir_ref[at, lane_tile(3 * chip + 2 * core)]
        out[rows:] = graft * fold(dir_ref[at, lane_tile(3 * chip + 1)], core)


def stats_kernel(tiles, shards, owner_ref, ah_ref, al_ref, bh_ref, bl_ref, ch_ref, cl_ref, left_ref, right_ref, nl_ref, nr_ref, gh_ref, gl_ref):
    shard, t, chip, core = place()
    rows = left_ref.shape[1]
    half = ah_ref.shape[0]
    side = shard // (shards // 2)

    def part(index):
        return pl.ds(pl.multiple_of(index * half, half), half)

    for ref, a, b, c in ((gh_ref, ah_ref, bh_ref, ch_ref), (gl_ref, al_ref, bl_ref, cl_ref)):
        ref[part(side), :] = a[...]
        ref[part(1 - side), part(chip)] = b[...]
        ref[part(1 - side), part(1 - chip)] = c[...]
    held = owner_ref[0] == shard
    for i in range(1, tiles):
        held = jnp.logical_or(held, owner_ref[i] == shard)

    def three(high, low, dims):
        dot = functools.partial(lax.dot_general, dimension_numbers=(dims, ((), ())), preferred_element_type=F32)
        return dot(high, gh_ref[...]) + dot(high, gl_ref[...]) + dot(low, gh_ref[...])

    def refreshed(old, new):
        return STAT_DECAY * old + (1.0 - STAT_DECAY) * jnp.where(held, new, 0.0)

    at = pl.ds(pl.multiple_of(t * rows, rows), rows)
    nl_ref[0] = refreshed(left_ref[0], three(gh_ref[at, :], gl_ref[at, :], ((1,), (1,))))
    end, mid = lane_tile(3 * chip + 2 * core), lane_tile(3 * chip + 1)
    ends = three(gh_ref[:, end], gl_ref[:, end], ((0,), (0,)))
    mids = three(gh_ref[:, mid], gl_ref[:, mid], ((0,), (0,)))
    half = LANES // 2

    @pl.when(core == 0)
    def _():
        nr_ref[0, :LANES] = refreshed(right_ref[0, :LANES], ends)
        nr_ref[0, LANES:] = refreshed(right_ref[0, LANES:], mids[:half])

    @pl.when(core == 1)
    def _():
        nr_ref[0, :half] = refreshed(right_ref[0, :half], mids[half:])
        nr_ref[0, half:] = refreshed(right_ref[0, half:], ends)


def back_kernel(rows, tiles, shards, owner_ref, *refs):
    blocks, out_ref = refs[:shards], refs[shards]
    shard, _, _, core = place()
    for j, block in zip(BACK, blocks):
        k = tile_of(owner_ref, shard ^ j, tiles)

        @pl.when(owner_ref[k] == (shard ^ j))
        def _(k=k, block=block):
            out_ref[k, :, :LANES], out_ref[k, :, LANES:] = unfold(block[...], rows, core)


def shape(dims, dtype=F32):
    return jax.ShapeDtypeStruct(dims, dtype)


def kernel_call(body, outs, ins, scratch=(), smem=0, flops=0, mib=16):
    vmem = pl.BlockSpec(memory_space=pltpu.VMEM)
    moved = sum(a.size * a.dtype.itemsize for a in (*ins, *jax.tree.leaves(outs)))
    return pl.pallas_call(
        body,
        out_shape=outs,
        in_specs=[pl.BlockSpec(memory_space=pltpu.SMEM)] * smem + [vmem] * (len(ins) - smem),
        out_specs=jax.tree.map(lambda _: vmem, outs),
        scratch_shapes=list(scratch),
        compiler_params=pltpu.CompilerParams(vmem_limit_bytes=mib << 20),
        cost_estimate=pl.CostEstimate(flops=flops, bytes_accessed=moved, transcendentals=0),
    )(*ins)


def swap(a, axis, mask):
    return lax.ppermute(a, axis, [(i, i ^ mask) for i in range(lax.axis_size(axis))])


def local(
    grad_parts, adam_v, left_stat, right_stat, left_root, right_root, owner, vec_parts, vec_m, vec_v
):
    shards = lax.axis_size("shard")
    tiles, rows, cols = adam_v.shape
    size = grad_parts.shape[3]
    packed = rows + rows // 2

    block = shape((tiles * packed, LANES))
    wide = shape((tiles * packed + EXTRA, LANES))
    sf, kf = kernel_call(functools.partial(split_kernel, rows, tiles, True), (block, block), (grad_parts,))
    sn, kn = kernel_call(functools.partial(split_kernel, rows, tiles, False), (wide, wide), (grad_parts, vec_parts))
    u = kf + swap(sf, "tensor", 1)
    rn = swap(sn, "tensor", 1)
    r = swap(u, "tensor", 2)
    roots = jnp.concatenate([left_root, right_root], axis=0)
    quadrant = lax.axis_index("tensor") // 2 * (size // 2)
    crossing = lax.dynamic_slice_in_dim(roots, quadrant, size // 2, 2)
    roots_core = swap(roots, "tensor", 1)
    r, roots, roots_core, crossing = lax.optimization_barrier((r, roots, roots_core, crossing))
    res = kernel_call(
        functools.partial(adam_kernel, rows, tiles, shards),
        (shape((packed + EXTRA, LANES)),) * shards + (shape(adam_v.shape), shape((EXTRA, LANES))),
        (owner, kn, rn, r, adam_v),
        (pltpu.VMEM((tiles, packed, LANES), F32), pltpu.VMEM((tiles, EXTRA, LANES), F32)),
        smem=1,
    )
    outgoing, (adam_new, vec_pair) = res[:shards], res[shards:]

    arrived = [outgoing[0]] + [swap(outgoing[j], "shard", j) for j in range(1, shards)]
    crossing, vec_pair = lax.optimization_barrier((crossing, vec_pair))
    roots_chip = swap(crossing, "tensor", 2)
    near = jnp.concatenate([*arrived[: shards // 2], vec_pair], axis=0)
    far = jnp.concatenate(arrived[shards // 2 :], axis=0)
    near, roots_chip = lax.optimization_barrier((near, roots_chip))
    full = shape((size, size), BF16)
    left_full, right_full = kernel_call(
        roots_kernel, (full, full), (roots, roots_core, roots_chip, swap(roots_chip, "tensor", 1)), mib=24
    )
    near_across = swap(near, "tensor", 2)
    near = near, swap(near, "tensor", 1), near_across, swap(near_across, "tensor", 1)
    far_across = swap(far, "tensor", 2)
    half = size // 2
    tall, square = shape((half, size), BF16), shape((half, half), BF16)
    vec = shape(vec_m.shape)
    ah, al, bh, bl, z, part, adam, new_vec_m, new_vec_v, vec_step, new_adam_v = kernel_call(
        functools.partial(near_kernel, rows, shards),
        (tall, tall, square, square, shape((half, size)), shape((size, size)), shape((EXTRA, LANES)), vec, vec, vec, shape(adam_v.shape)),
        (*near, far, swap(far, "tensor", 1), left_full, right_full, vec_m, vec_v, adam_new),
        (pltpu.VMEM((half, size), BF16),) * 2,
        flops=5 * size**3,
        mib=32,
    )
    far_across, adam = lax.optimization_barrier((far_across, adam))
    ch, cl, *ready = kernel_call(
        functools.partial(owner_kernel, rows, shards),
        (square, square) + (shape((packed, LANES)),) * shards,
        (far_across, swap(far_across, "tensor", 1), z, part, adam, left_full, right_full),
        (pltpu.VMEM((half, size), BF16),) * 2 + (pltpu.VMEM((size, size), F32),),
        flops=3 * size**3,
        mib=32,
    )
    back = [swap(block, "shard", j) if j else block for j, block in zip(BACK, ready)]
    new_left, new_right = kernel_call(
        functools.partial(stats_kernel, tiles, shards),
        (shape(left_stat.shape), shape(right_stat.shape)),
        (owner, ah, al, bh, bl, ch, cl, left_stat, right_stat),
        (pltpu.VMEM((size, size), BF16),) * 2,
        smem=1,
        flops=12 * cols * size**2,
        mib=32,
    )
    update = kernel_call(
        functools.partial(back_kernel, rows, tiles, shards), shape(adam_v.shape), (owner, *back), smem=1
    )
    return (update, new_adam_v, new_left, new_right, new_vec_m, new_vec_v, vec_step)


def solution(mesh):
    in_specs = (
        P("tensor", None, "shard", None),
        P(None, "shard", "tensor"),
        P("shard", "tensor", None),
        P("shard", "tensor", None),
        P("shard", "tensor", None),
        P("shard", "tensor", None),
        P(),
        P("tensor", None, "shard"),
        P(None, "shard"),
        P(None, "shard"),
    )
    out_specs = (
        P(None, "shard", "tensor"),
        P(None, "shard", "tensor"),
        P("shard", "tensor", None),
        P("shard", "tensor", None),
        P(None, "shard"),
        P(None, "shard"),
        P(None, "shard"),
    )
    packs = mesh.shape["tensor"] == 4 and mesh.shape["shard"] == 8
    return jax.shard_map(
        local if packs else plain, mesh=mesh, in_specs=in_specs, out_specs=out_specs, check_vma=False
    )
```

```python
import functools

import jax
import jax.numpy as jnp
from jax import lax
from jax.experimental import pallas as pl
from jax.experimental.pallas import tpu as pltpu
from jax.sharding import PartitionSpec as P

BETA_ONE = 0.9
BETA_TWO = 0.95
STAT_DECAY = 0.95
STEP_COUNT = 10.0
EPSILON = 1e-08
NORM_EPS = 1e-06
BIAS_ONE = 1.0 - BETA_ONE**STEP_COUNT
BIAS_TWO = 1.0 - BETA_TWO**STEP_COUNT
HIGH = lax.Precision.HIGHEST
LANES = 128
BACK = (4, 1, 5, 2, 6, 3, 7, 0)
EXTRA = 8
F32 = jnp.float32
BF16 = jnp.bfloat16


def plain(
    grad_parts, adam_v, left_stat, right_stat, left_root, right_root, owner, vec_parts, vec_m, vec_v
):
    shards = lax.axis_size("shard")
    tiles = owner.shape[0]
    grad = lax.psum_scatter(grad_parts[0], "tensor", scatter_dimension=2, tiled=True)
    rows_dev = grad.shape[1]
    cols_dev = grad.shape[2]
    new_adam_v = BETA_TWO * adam_v + (1.0 - BETA_TWO) * grad * grad
    adam_dir = grad / (jnp.sqrt(new_adam_v / BIAS_TWO) + EPSILON)
    adam_sq = jnp.sum(adam_dir * adam_dir, axis=(1, 2))
    vec_grad = lax.psum(vec_parts[0], "tensor")
    new_vec_m, new_vec_v, vec_step = vec_update(vec_grad, vec_m, vec_v)
    slot_hot = (jnp.arange(shards, dtype=jnp.int32)[:, None] == owner[None, :]).astype(F32)
    outgoing = jnp.dot(slot_hot, grad.reshape(tiles, rows_dev * cols_dev), precision=HIGH)
    outgoing = outgoing.reshape(shards, rows_dev, cols_dev)
    arrived = lax.all_to_all(outgoing, "shard", split_axis=0, concat_axis=1, tiled=True)[0]
    whole = lax.all_gather(arrived, "tensor", axis=1, tiled=True)
    start = lax.axis_index("tensor") * cols_dev
    tile_rows = lax.dynamic_slice_in_dim(whole, start, cols_dev, 0)
    new_left = STAT_DECAY * left_stat[0] + (1.0 - STAT_DECAY) * jnp.dot(
        tile_rows, whole.T, precision=HIGH
    )
    new_right = STAT_DECAY * right_stat[0] + (1.0 - STAT_DECAY) * jnp.dot(
        arrived.T, whole, precision=HIGH
    )
    left_full = lax.all_gather(left_root[0], "tensor", axis=0, tiled=True).astype(F32)
    right_part = jnp.dot(whole, right_root[0].astype(F32).T, precision=HIGH)
    direction = jnp.dot(left_full, right_part, precision=HIGH)
    returned = lax.all_to_all(
        direction.reshape(shards, rows_dev, cols_dev),
        "shard",
        split_axis=0,
        concat_axis=0,
        tiled=True,
    )
    update = jnp.dot(slot_hot.T, returned.reshape(shards, rows_dev * cols_dev), precision=HIGH)
    update = update.reshape(tiles, rows_dev, cols_dev)
    shampoo_local = jnp.sum(update * update, axis=(1, 2))
    adam_total, shampoo_total = lax.psum((adam_sq, shampoo_local), ("shard", "tensor"))
    graft = jnp.sqrt(adam_total) / (jnp.sqrt(shampoo_total) + NORM_EPS)
    update = graft[:, None, None] * update
    return (update, new_adam_v, new_left[None], new_right[None], new_vec_m, new_vec_v, vec_step)


def vec_update(vec_grad, vec_m, vec_v):
    new_vec_m = BETA_ONE * vec_m + (1.0 - BETA_ONE) * vec_grad
    new_vec_v = BETA_TWO * vec_v + (1.0 - BETA_TWO) * vec_grad * vec_grad
    vec_step = new_vec_m / BIAS_ONE / (jnp.sqrt(new_vec_v / BIAS_TWO) + EPSILON)
    return new_vec_m, new_vec_v, vec_step


def place():
    t = lax.axis_index("tensor")
    return lax.axis_index("shard"), t, t // 2, lax.rem(t, 2)


def lane_tile(index):
    return pl.ds(pl.multiple_of(index * LANES, LANES), LANES)


def swap_halves(a):
    return pltpu.roll(a, LANES // 2, 1)


def low_lanes(rows):
    return lax.broadcasted_iota(jnp.int32, (rows, LANES), 1) < LANES // 2


def fold(mid, core):
    half = mid.shape[0] // 2
    turned = swap_halves(mid)
    first = core == 0
    low = low_lanes(half)
    top = jnp.where(first, mid[:half], turned[:half])
    bottom = jnp.where(first, turned[half:], mid[half:])
    return jnp.where(low, top, bottom)


def unfold(block, rows, core):
    main, side = block[:rows], block[rows:]
    wide = jnp.concatenate([side, swap_halves(side)], axis=0)
    turned = swap_halves(main)
    first = core == 0
    head = jnp.where(first, main, jnp.where(low_lanes(rows), wide, turned))
    return head, jnp.where(first, wide, turned)[:, : LANES // 2]


def split_kernel(rows, tiles, far, g_ref, *refs):
    vec_ref, send_ref, keep_ref = refs if len(refs) == 3 else (None, *refs)
    _, _, chip, core = place()
    packed = rows + rows // 2
    x = 1 - chip if far else chip
    for out, d in ((send_ref, 1 - core), (keep_ref, core)):
        for k in range(tiles):
            base = k * packed
            out[base : base + rows] = g_ref[0, k, :, lane_tile(3 * x + 2 * d)]
            out[base + rows : base + packed] = fold(g_ref[0, k, :, lane_tile(3 * x + 1)], d)
        if vec_ref is not None:
            out[tiles * packed :] = jnp.zeros((EXTRA, LANES), F32)
            out[tiles * packed : tiles * packed + tiles, :rows] = vec_ref[0]


def tile_of(owner_ref, slot, tiles):
    k = jnp.int32(0)
    for i in range(1, tiles):
        k = jnp.where(owner_ref[i] == slot, i, k)
    return k


def adam_kernel(
    rows, tiles, shards, owner_ref, kn_ref, rn_ref, r_ref, v_ref, *refs
):
    outs, (nv_ref, vec_ref, g_ref, ext_ref) = refs[:shards], refs[shards:]
    shard, _, _, core = place()
    packed = rows + rows // 2

    def one(g, v_old):
        v_new = BETA_TWO * v_old + (1.0 - BETA_TWO) * g * g
        step = g / (jnp.sqrt(v_new * (1.0 / BIAS_TWO)) + EPSILON)
        sq = step * step
        return v_new, jnp.sum(sq.reshape(-1, 8, sq.shape[1]), axis=0)

    for k in range(tiles):
        at = slice(k * packed, k * packed + packed)
        g = kn_ref[at] + rn_ref[at] + r_ref[at]
        g_ref[k] = g
        head, tail = unfold(g, rows, core)
        nv_ref[k, :, :LANES], ext_ref[k] = one(head, v_ref[k, :, :LANES])
        nv_ref[k, :, LANES:], sq = one(tail, v_ref[k, :, LANES:])
        ext_ref[k, :, : LANES // 2] += sq
    for j in range(shards):
        k = tile_of(owner_ref, shard ^ j, tiles)
        outs[j][:packed] = g_ref[k]
        outs[j][packed:] = ext_ref[k]
    vec_ref[...] = kn_ref[tiles * packed :] + rn_ref[tiles * packed :]


def roots_kernel(own_ref, core_ref, chip_ref, both_ref, left_ref, right_ref):
    _, t, chip, _ = place()
    rows, size = own_ref.shape[1], left_ref.shape[0]
    half = size // 2
    here = pl.ds(pl.multiple_of(chip * half, half), half)
    there = pl.ds(pl.multiple_of((1 - chip) * half, half), half)

    def block(mask):
        return pl.ds(pl.multiple_of((t ^ mask) * rows, rows), rows)

    for n, ref in enumerate((left_ref, right_ref)):
        ref[block(0), :] = own_ref[n]
        ref[block(1), :] = core_ref[n]
        ref[block(2), there] = chip_ref[n]
        ref[block(3), there] = both_ref[n]
        ref[there, here] = ref[here, there].T


def halves(a):
    high = a.astype(BF16)
    return high, (a - high.astype(F32)).astype(BF16)


def laid_out(mine, peer, i, rows, core):
    packed = rows + rows // 2
    base = i * (packed + EXTRA)
    a, b = mine[base : base + packed], peer[base : base + packed]
    extra = mine[base + packed : base + packed + EXTRA] + peer[base + packed : base + packed + EXTRA]
    first, last = jnp.where(core == 0, a, b), jnp.where(core == 0, b, a)
    fs, ls = first[rows:], last[rows:]
    low = low_lanes(rows // 2)
    mid = jnp.concatenate([jnp.where(low, fs, swap_halves(ls)), jnp.where(low, swap_halves(fs), ls)], axis=0)
    return (first[:rows], mid, last[:rows]), extra


def product(a, b):
    return jnp.dot(a, b, preferred_element_type=F32)


def near_kernel(
    rows, shards, mine_ref, peer_ref, chip_ref, both_ref, far_ref, far_peer_ref, left_ref, right_ref,
    m_ref, v_ref, adam_new, ah_ref, al_ref, bh_ref, bl_ref, z_ref, dir_ref, adam_ref, nm_ref, nv_ref, step_ref,
    adam_out, zh_ref, zl_ref
):
    shard, _, chip, core = place()
    group = shards // 2
    half = group * rows
    adam = jnp.zeros((EXTRA, LANES), F32)
    for i in range(group):
        to = pl.ds(pl.multiple_of((lax.rem(shard, group) ^ i) * rows, rows), rows)
        for x, mine, peer in ((chip, mine_ref, peer_ref), (1 - chip, chip_ref, both_ref)):
            parts, extra = laid_out(mine, peer, i, rows, core)
            adam += extra
            for n, tile in enumerate(parts):
                ah_ref[to, lane_tile(3 * x + n)], al_ref[to, lane_tile(3 * x + n)] = halves(tile)
        parts, extra = laid_out(far_ref, far_peer_ref, i, rows, core)
        adam += extra
        for n, tile in enumerate(parts):
            bh_ref[to, n * LANES : (n + 1) * LANES], bl_ref[to, n * LANES : (n + 1) * LANES] = halves(tile)
    adam_ref[...] = adam
    end = group * (rows + rows // 2 + EXTRA)
    vecs, wide = m_ref.shape
    vec = mine_ref[end : end + vecs, :wide] + chip_ref[end : end + vecs, :wide]
    nm_ref[...], nv_ref[...], step_ref[...] = vec_update(vec, m_ref[...], v_ref[...])
    adam_out[...] = adam_new[...]
    z = product(ah_ref[...], right_ref[...]) + product(al_ref[...], right_ref[...])
    zh_ref[...], zl_ref[...] = halves(z)
    here = pl.ds(pl.multiple_of(chip * half, half), half)
    z_ref[...] = product(bh_ref[...], right_ref[here, :]) + product(bl_ref[...], right_ref[here, :])
    near = pl.ds(pl.multiple_of(shard // group * half, half), half)
    for n in range(2):
        at = slice(n * half, (n + 1) * half)
        dir_ref[at] = product(left_ref[at, near], zh_ref[...]) + product(left_ref[at, near], zl_ref[...])


def owner_kernel(rows, shards, chip_ref, both_ref, z_ref, part_ref, adam_ref, left_ref, right_ref, *refs):
    (bh_ref, bl_ref), outs, (zh_ref, zl_ref, dir_ref) = refs[:2], refs[2 : shards + 2], refs[shards + 2 :]
    shard, _, chip, core = place()
    group = shards // 2
    half = group * rows
    adam = adam_ref[...]
    for i in range(group):
        to = pl.ds(pl.multiple_of((lax.rem(shard, group) ^ i) * rows, rows), rows)
        parts, extra = laid_out(chip_ref, both_ref, i, rows, core)
        adam += extra
        for n, tile in enumerate(parts):
            bh_ref[to, n * LANES : (n + 1) * LANES], bl_ref[to, n * LANES : (n + 1) * LANES] = halves(tile)
    there = pl.ds(pl.multiple_of((1 - chip) * half, half), half)
    z = z_ref[...] + product(bh_ref[...], right_ref[there, :]) + product(bl_ref[...], right_ref[there, :])
    zh_ref[...], zl_ref[...] = halves(z)
    far = pl.ds(pl.multiple_of((1 - shard // group) * half, half), half)
    squares = jnp.zeros((8, 2 * half), F32)
    for n in range(2):
        at = slice(n * half, (n + 1) * half)
        d = part_ref[at] + product(left_ref[at, far], zh_ref[...]) + product(left_ref[at, far], zl_ref[...])
        dir_ref[at] = d
        squares += jnp.sum((d * d).reshape(-1, 8, 2 * half), axis=0)

    def whole(a):
        return jnp.sum(jnp.sum(a, axis=1, keepdims=True), axis=0, keepdims=True)

    graft = jnp.sqrt(whole(adam)) / (jnp.sqrt(whole(squares)) + NORM_EPS)
    for j, out in zip(BACK, outs):
        at = pl.ds(pl.multiple_of((shard ^ j) * rows, rows), rows)
        out[:rows] = graft * dir_ref[at, lane_tile(3 * chip + 2 * core)]
        out[rows:] = graft * fold(dir_ref[at, lane_tile(3 * chip + 1)], core)


def stats_kernel(tiles, shards, owner_ref, ah_ref, al_ref, bh_ref, bl_ref, ch_ref, cl_ref, left_ref, right_ref, nl_ref, nr_ref, gh_ref, gl_ref):
    shard, t, chip, core = place()
    rows = left_ref.shape[1]
    half = ah_ref.shape[0]
    side = shard // (shards // 2)

    def part(index):
        return pl.ds(pl.multiple_of(index * half, half), half)

    for ref, a, b, c in ((gh_ref, ah_ref, bh_ref, ch_ref), (gl_ref, al_ref, bl_ref, cl_ref)):
        ref[part(side), :] = a[...]
        ref[part(1 - side), part(chip)] = b[...]
        ref[part(1 - side), part(1 - chip)] = c[...]
    held = owner_ref[0] == shard
    for i in range(1, tiles):
        held = jnp.logical_or(held, owner_ref[i] == shard)

    def three(high, low, dims):
        dot = functools.partial(lax.dot_general, dimension_numbers=(dims, ((), ())), preferred_element_type=F32)
        return dot(high, gh_ref[...]) + dot(high, gl_ref[...]) + dot(low, gh_ref[...])

    def refreshed(old, new):
        return STAT_DECAY * old + (1.0 - STAT_DECAY) * jnp.where(held, new, 0.0)

    at = pl.ds(pl.multiple_of(t * rows, rows), rows)
    nl_ref[0] = refreshed(left_ref[0], three(gh_ref[at, :], gl_ref[at, :], ((1,), (1,))))
    end, mid = lane_tile(3 * chip + 2 * core), lane_tile(3 * chip + 1)
    ends = three(gh_ref[:, end], gl_ref[:, end], ((0,), (0,)))
    mids = three(gh_ref[:, mid], gl_ref[:, mid], ((0,), (0,)))
    half = LANES // 2

    @pl.when(core == 0)
    def _():
        nr_ref[0, :LANES] = refreshed(right_ref[0, :LANES], ends)
        nr_ref[0, LANES:] = refreshed(right_ref[0, LANES:], mids[:half])

    @pl.when(core == 1)
    def _():
        nr_ref[0, :half] = refreshed(right_ref[0, :half], mids[half:])
        nr_ref[0, half:] = refreshed(right_ref[0, half:], ends)


def back_kernel(rows, tiles, shards, owner_ref, *refs):
    blocks, out_ref = refs[:shards], refs[shards]
    shard, _, _, core = place()
    for j, block in zip(BACK, blocks):
        k = tile_of(owner_ref, shard ^ j, tiles)

        @pl.when(owner_ref[k] == (shard ^ j))
        def _(k=k, block=block):
            out_ref[k, :, :LANES], out_ref[k, :, LANES:] = unfold(block[...], rows, core)


def shape(dims, dtype=F32):
    return jax.ShapeDtypeStruct(dims, dtype)


def kernel_call(body, outs, ins, scratch=(), smem=0, flops=0, mib=16):
    vmem = pl.BlockSpec(memory_space=pltpu.VMEM)
    moved = sum(a.size * a.dtype.itemsize for a in (*ins, *jax.tree.leaves(outs)))
    return pl.pallas_call(
        body,
        out_shape=outs,
        in_specs=[pl.BlockSpec(memory_space=pltpu.SMEM)] * smem + [vmem] * (len(ins) - smem),
        out_specs=jax.tree.map(lambda _: vmem, outs),
        scratch_shapes=list(scratch),
        compiler_params=pltpu.CompilerParams(vmem_limit_bytes=mib << 20),
        cost_estimate=pl.CostEstimate(flops=flops, bytes_accessed=moved, transcendentals=0),
    )(*ins)


def swap(a, axis, mask):
    return lax.ppermute(a, axis, [(i, i ^ mask) for i in range(lax.axis_size(axis))])


def local(
    grad_parts, adam_v, left_stat, right_stat, left_root, right_root, owner, vec_parts, vec_m, vec_v
):
    shards = lax.axis_size("shard")
    tiles, rows, cols = adam_v.shape
    size = grad_parts.shape[3]
    packed = rows + rows // 2

    block = shape((tiles * packed, LANES))
    wide = shape((tiles * packed + EXTRA, LANES))
    sf, kf = kernel_call(functools.partial(split_kernel, rows, tiles, True), (block, block), (grad_parts,))
    sn, kn = kernel_call(functools.partial(split_kernel, rows, tiles, False), (wide, wide), (grad_parts, vec_parts))
    u = kf + swap(sf, "tensor", 1)
    rn = swap(sn, "tensor", 1)
    r = swap(u, "tensor", 2)
    roots = jnp.concatenate([left_root, right_root], axis=0)
    quadrant = lax.axis_index("tensor") // 2 * (size // 2)
    crossing = lax.dynamic_slice_in_dim(roots, quadrant, size // 2, 2)
    roots_core = swap(roots, "tensor", 1)
    r, roots, roots_core, crossing = lax.optimization_barrier((r, roots, roots_core, crossing))
    res = kernel_call(
        functools.partial(adam_kernel, rows, tiles, shards),
        (shape((packed + EXTRA, LANES)),) * shards + (shape(adam_v.shape), shape((EXTRA, LANES))),
        (owner, kn, rn, r, adam_v),
        (pltpu.VMEM((tiles, packed, LANES), F32), pltpu.VMEM((tiles, EXTRA, LANES), F32)),
        smem=1,
    )
    outgoing, (adam_new, vec_pair) = res[:shards], res[shards:]

    arrived = [outgoing[0]] + [swap(outgoing[j], "shard", j) for j in range(1, shards)]
    crossing, vec_pair = lax.optimization_barrier((crossing, vec_pair))
    roots_chip = swap(crossing, "tensor", 2)
    near = jnp.concatenate([*arrived[: shards // 2], vec_pair], axis=0)
    far = jnp.concatenate(arrived[shards // 2 :], axis=0)
    near, roots_chip = lax.optimization_barrier((near, roots_chip))
    near_across = swap(near, "tensor", 2)
    near_across, roots_both = lax.optimization_barrier((near_across, swap(roots_chip, "tensor", 1)))
    full = shape((size, size), BF16)
    left_full, right_full = kernel_call(
        roots_kernel, (full, full), (roots, roots_core, roots_chip, roots_both), mib=24
    )
    near = near, swap(near, "tensor", 1), near_across, swap(near_across, "tensor", 1)
    far_across = swap(far, "tensor", 2)
    half = size // 2
    tall, square = shape((half, size), BF16), shape((half, half), BF16)
    vec = shape(vec_m.shape)
    ah, al, bh, bl, z, part, adam, new_vec_m, new_vec_v, vec_step, new_adam_v = kernel_call(
        functools.partial(near_kernel, rows, shards),
        (tall, tall, square, square, shape((half, size)), shape((size, size)), shape((EXTRA, LANES)), vec, vec, vec, shape(adam_v.shape)),
        (*near, far, swap(far, "tensor", 1), left_full, right_full, vec_m, vec_v, adam_new),
        (pltpu.VMEM((half, size), BF16),) * 2,
        flops=5 * size**3,
        mib=32,
    )
    far_across, adam = lax.optimization_barrier((far_across, adam))
    ch, cl, *ready = kernel_call(
        functools.partial(owner_kernel, rows, shards),
        (square, square) + (shape((packed, LANES)),) * shards,
        (far_across, swap(far_across, "tensor", 1), z, part, adam, left_full, right_full),
        (pltpu.VMEM((half, size), BF16),) * 2 + (pltpu.VMEM((size, size), F32),),
        flops=3 * size**3,
        mib=32,
    )
    back = [swap(block, "shard", j) if j else block for j, block in zip(BACK, ready)]
    new_left, new_right = kernel_call(
        functools.partial(stats_kernel, tiles, shards),
        (shape(left_stat.shape), shape(right_stat.shape)),
        (owner, ah, al, bh, bl, ch, cl, left_stat, right_stat),
        (pltpu.VMEM((size, size), BF16),) * 2,
        smem=1,
        flops=12 * cols * size**2,
        mib=32,
    )
    update = kernel_call(
        functools.partial(back_kernel, rows, tiles, shards), shape(adam_v.shape), (owner, *back), smem=1
    )
    return (update, new_adam_v, new_left, new_right, new_vec_m, new_vec_v, vec_step)


def solution(mesh):
    in_specs = (
        P("tensor", None, "shard", None),
        P(None, "shard", "tensor"),
        P("shard", "tensor", None),
        P("shard", "tensor", None),
        P("shard", "tensor", None),
        P("shard", "tensor", None),
        P(),
        P("tensor", None, "shard"),
        P(None, "shard"),
        P(None, "shard"),
    )
    out_specs = (
        P(None, "shard", "tensor"),
        P(None, "shard", "tensor"),
        P("shard", "tensor", None),
        P("shard", "tensor", None),
        P(None, "shard"),
        P(None, "shard"),
        P(None, "shard"),
    )
    packs = mesh.shape["tensor"] == 4 and mesh.shape["shard"] == 8
    return jax.shard_map(
        local if packs else plain, mesh=mesh, in_specs=in_specs, out_specs=out_specs, check_vma=False
    )
```

```python
import functools

import jax
import jax.numpy as jnp
from jax import lax
from jax.experimental import pallas as pl
from jax.experimental.pallas import tpu as pltpu
from jax.sharding import PartitionSpec as P

BETA_ONE = 0.9
BETA_TWO = 0.95
STAT_DECAY = 0.95
STEP_COUNT = 10.0
EPSILON = 1e-08
NORM_EPS = 1e-06
BIAS_ONE = 1.0 - BETA_ONE**STEP_COUNT
BIAS_TWO = 1.0 - BETA_TWO**STEP_COUNT
HIGH = lax.Precision.HIGHEST
LANES = 128
BACK = (4, 1, 5, 3, 6, 2, 7, 0)
EXTRA = 8
F32 = jnp.float32
BF16 = jnp.bfloat16


def plain(
    grad_parts, adam_v, left_stat, right_stat, left_root, right_root, owner, vec_parts, vec_m, vec_v
):
    shards = lax.axis_size("shard")
    tiles = owner.shape[0]
    grad = lax.psum_scatter(grad_parts[0], "tensor", scatter_dimension=2, tiled=True)
    rows_dev = grad.shape[1]
    cols_dev = grad.shape[2]
    new_adam_v = BETA_TWO * adam_v + (1.0 - BETA_TWO) * grad * grad
    adam_dir = grad / (jnp.sqrt(new_adam_v / BIAS_TWO) + EPSILON)
    adam_sq = jnp.sum(adam_dir * adam_dir, axis=(1, 2))
    vec_grad = lax.psum(vec_parts[0], "tensor")
    new_vec_m, new_vec_v, vec_step = vec_update(vec_grad, vec_m, vec_v)
    slot_hot = (jnp.arange(shards, dtype=jnp.int32)[:, None] == owner[None, :]).astype(F32)
    outgoing = jnp.dot(slot_hot, grad.reshape(tiles, rows_dev * cols_dev), precision=HIGH)
    outgoing = outgoing.reshape(shards, rows_dev, cols_dev)
    arrived = lax.all_to_all(outgoing, "shard", split_axis=0, concat_axis=1, tiled=True)[0]
    whole = lax.all_gather(arrived, "tensor", axis=1, tiled=True)
    start = lax.axis_index("tensor") * cols_dev
    tile_rows = lax.dynamic_slice_in_dim(whole, start, cols_dev, 0)
    new_left = STAT_DECAY * left_stat[0] + (1.0 - STAT_DECAY) * jnp.dot(
        tile_rows, whole.T, precision=HIGH
    )
    new_right = STAT_DECAY * right_stat[0] + (1.0 - STAT_DECAY) * jnp.dot(
        arrived.T, whole, precision=HIGH
    )
    left_full = lax.all_gather(left_root[0], "tensor", axis=0, tiled=True).astype(F32)
    right_part = jnp.dot(whole, right_root[0].astype(F32).T, precision=HIGH)
    direction = jnp.dot(left_full, right_part, precision=HIGH)
    returned = lax.all_to_all(
        direction.reshape(shards, rows_dev, cols_dev),
        "shard",
        split_axis=0,
        concat_axis=0,
        tiled=True,
    )
    update = jnp.dot(slot_hot.T, returned.reshape(shards, rows_dev * cols_dev), precision=HIGH)
    update = update.reshape(tiles, rows_dev, cols_dev)
    shampoo_local = jnp.sum(update * update, axis=(1, 2))
    adam_total, shampoo_total = lax.psum((adam_sq, shampoo_local), ("shard", "tensor"))
    graft = jnp.sqrt(adam_total) / (jnp.sqrt(shampoo_total) + NORM_EPS)
    update = graft[:, None, None] * update
    return (update, new_adam_v, new_left[None], new_right[None], new_vec_m, new_vec_v, vec_step)


def vec_update(vec_grad, vec_m, vec_v):
    new_vec_m = BETA_ONE * vec_m + (1.0 - BETA_ONE) * vec_grad
    new_vec_v = BETA_TWO * vec_v + (1.0 - BETA_TWO) * vec_grad * vec_grad
    vec_step = new_vec_m / BIAS_ONE / (jnp.sqrt(new_vec_v / BIAS_TWO) + EPSILON)
    return new_vec_m, new_vec_v, vec_step


def place():
    t = lax.axis_index("tensor")
    return lax.axis_index("shard"), t, t // 2, lax.rem(t, 2)


def lane_tile(index):
    return pl.ds(pl.multiple_of(index * LANES, LANES), LANES)


def swap_halves(a):
    return pltpu.roll(a, LANES // 2, 1)


def low_lanes(rows):
    return lax.broadcasted_iota(jnp.int32, (rows, LANES), 1) < LANES // 2


def fold(mid, core):
    half = mid.shape[0] // 2
    turned = swap_halves(mid)
    first = core == 0
    low = low_lanes(half)
    top = jnp.where(first, mid[:half], turned[:half])
    bottom = jnp.where(first, turned[half:], mid[half:])
    return jnp.where(low, top, bottom)


def unfold(block, rows, core):
    main, side = block[:rows], block[rows:]
    wide = jnp.concatenate([side, swap_halves(side)], axis=0)
    turned = swap_halves(main)
    first = core == 0
    head = jnp.where(first, main, jnp.where(low_lanes(rows), wide, turned))
    return head, jnp.where(first, wide, turned)[:, : LANES // 2]


def split_kernel(rows, tiles, far, g_ref, *refs):
    vec_ref, send_ref, keep_ref = refs if len(refs) == 3 else (None, *refs)
    _, _, chip, core = place()
    packed = rows + rows // 2
    x = 1 - chip if far else chip
    for out, d in ((send_ref, 1 - core), (keep_ref, core)):
        for k in range(tiles):
            base = k * packed
            out[base : base + rows] = g_ref[0, k, :, lane_tile(3 * x + 2 * d)]
            out[base + rows : base + packed] = fold(g_ref[0, k, :, lane_tile(3 * x + 1)], d)
        if vec_ref is not None:
            out[tiles * packed :] = jnp.zeros((EXTRA, LANES), F32)
            out[tiles * packed : tiles * packed + tiles, :rows] = vec_ref[0]


def tile_of(owner_ref, slot, tiles):
    k = jnp.int32(0)
    for i in range(1, tiles):
        k = jnp.where(owner_ref[i] == slot, i, k)
    return k


def adam_kernel(
    rows, tiles, shards, owner_ref, kn_ref, rn_ref, r_ref, v_ref, *refs
):
    outs, (nv_ref, vec_ref, g_ref, ext_ref) = refs[:shards], refs[shards:]
    shard, _, _, core = place()
    packed = rows + rows // 2

    def one(g, v_old):
        v_new = BETA_TWO * v_old + (1.0 - BETA_TWO) * g * g
        step = g / (jnp.sqrt(v_new * (1.0 / BIAS_TWO)) + EPSILON)
        sq = step * step
        return v_new, jnp.sum(sq.reshape(-1, 8, sq.shape[1]), axis=0)

    for k in range(tiles):
        at = slice(k * packed, k * packed + packed)
        g = kn_ref[at] + rn_ref[at] + r_ref[at]
        g_ref[k] = g
        head, tail = unfold(g, rows, core)
        nv_ref[k, :, :LANES], ext_ref[k] = one(head, v_ref[k, :, :LANES])
        nv_ref[k, :, LANES:], sq = one(tail, v_ref[k, :, LANES:])
        ext_ref[k, :, : LANES // 2] += sq
    for j in range(shards):
        k = tile_of(owner_ref, shard ^ j, tiles)
        outs[j][:packed] = g_ref[k]
        outs[j][packed:] = ext_ref[k]
    vec_ref[...] = kn_ref[tiles * packed :] + rn_ref[tiles * packed :]


def roots_kernel(own_ref, core_ref, chip_ref, both_ref, left_ref, right_ref):
    _, t, chip, _ = place()
    rows, size = own_ref.shape[1], left_ref.shape[0]
    half = size // 2
    here = pl.ds(pl.multiple_of(chip * half, half), half)
    there = pl.ds(pl.multiple_of((1 - chip) * half, half), half)

    def block(mask):
        return pl.ds(pl.multiple_of((t ^ mask) * rows, rows), rows)

    for n, ref in enumerate((left_ref, right_ref)):
        ref[block(0), :] = own_ref[n]
        ref[block(1), :] = core_ref[n]
        ref[block(2), there] = chip_ref[n]
        ref[block(3), there] = both_ref[n]
        ref[there, here] = ref[here, there].T


def halves(a):
    high = a.astype(BF16)
    return high, (a - high.astype(F32)).astype(BF16)


def laid_out(mine, peer, i, rows, core):
    packed = rows + rows // 2
    base = i * (packed + EXTRA)
    a, b = mine[base : base + packed], peer[base : base + packed]
    extra = mine[base + packed : base + packed + EXTRA] + peer[base + packed : base + packed + EXTRA]
    first, last = jnp.where(core == 0, a, b), jnp.where(core == 0, b, a)
    fs, ls = first[rows:], last[rows:]
    low = low_lanes(rows // 2)
    mid = jnp.concatenate([jnp.where(low, fs, swap_halves(ls)), jnp.where(low, swap_halves(fs), ls)], axis=0)
    return (first[:rows], mid, last[:rows]), extra


def product(a, b):
    return jnp.dot(a, b, preferred_element_type=F32)


def near_kernel(
    rows, shards, mine_ref, peer_ref, chip_ref, both_ref, far_ref, far_peer_ref, left_ref, right_ref,
    m_ref, v_ref, adam_new, ah_ref, al_ref, bh_ref, bl_ref, z_ref, dir_ref, adam_ref, nm_ref, nv_ref, step_ref,
    adam_out, zh_ref, zl_ref
):
    shard, _, chip, core = place()
    group = shards // 2
    half = group * rows
    adam = jnp.zeros((EXTRA, LANES), F32)
    for i in range(group):
        to = pl.ds(pl.multiple_of((lax.rem(shard, group) ^ i) * rows, rows), rows)
        for x, mine, peer in ((chip, mine_ref, peer_ref), (1 - chip, chip_ref, both_ref)):
            parts, extra = laid_out(mine, peer, i, rows, core)
            adam += extra
            for n, tile in enumerate(parts):
                ah_ref[to, lane_tile(3 * x + n)], al_ref[to, lane_tile(3 * x + n)] = halves(tile)
        parts, extra = laid_out(far_ref, far_peer_ref, i, rows, core)
        adam += extra
        for n, tile in enumerate(parts):
            bh_ref[to, n * LANES : (n + 1) * LANES], bl_ref[to, n * LANES : (n + 1) * LANES] = halves(tile)
    adam_ref[...] = adam
    end = group * (rows + rows // 2 + EXTRA)
    vecs, wide = m_ref.shape
    vec = mine_ref[end : end + vecs, :wide] + chip_ref[end : end + vecs, :wide]
    nm_ref[...], nv_ref[...], step_ref[...] = vec_update(vec, m_ref[...], v_ref[...])
    adam_out[...] = adam_new[...]
    z = product(ah_ref[...], right_ref[...]) + product(al_ref[...], right_ref[...])
    zh_ref[...], zl_ref[...] = halves(z)
    here = pl.ds(pl.multiple_of(chip * half, half), half)
    z_ref[...] = product(bh_ref[...], right_ref[here, :]) + product(bl_ref[...], right_ref[here, :])
    near = pl.ds(pl.multiple_of(shard // group * half, half), half)
    for n in range(2):
        at = slice(n * half, (n + 1) * half)
        dir_ref[at] = product(left_ref[at, near], zh_ref[...]) + product(left_ref[at, near], zl_ref[...])


def owner_kernel(rows, shards, chip_ref, both_ref, z_ref, part_ref, adam_ref, left_ref, right_ref, *refs):
    (bh_ref, bl_ref), outs, (zh_ref, zl_ref, dir_ref) = refs[:2], refs[2 : shards + 2], refs[shards + 2 :]
    shard, _, chip, core = place()
    group = shards // 2
    half = group * rows
    adam = adam_ref[...]
    for i in range(group):
        to = pl.ds(pl.multiple_of((lax.rem(shard, group) ^ i) * rows, rows), rows)
        parts, extra = laid_out(chip_ref, both_ref, i, rows, core)
        adam += extra
        for n, tile in enumerate(parts):
            bh_ref[to, n * LANES : (n + 1) * LANES], bl_ref[to, n * LANES : (n + 1) * LANES] = halves(tile)
    there = pl.ds(pl.multiple_of((1 - chip) * half, half), half)
    z = z_ref[...] + product(bh_ref[...], right_ref[there, :]) + product(bl_ref[...], right_ref[there, :])
    zh_ref[...], zl_ref[...] = halves(z)
    far = pl.ds(pl.multiple_of((1 - shard // group) * half, half), half)
    squares = jnp.zeros((8, 2 * half), F32)
    for n in range(2):
        at = slice(n * half, (n + 1) * half)
        d = part_ref[at] + product(left_ref[at, far], zh_ref[...]) + product(left_ref[at, far], zl_ref[...])
        dir_ref[at] = d
        squares += jnp.sum((d * d).reshape(-1, 8, 2 * half), axis=0)

    def whole(a):
        return jnp.sum(jnp.sum(a, axis=1, keepdims=True), axis=0, keepdims=True)

    graft = jnp.sqrt(whole(adam)) / (jnp.sqrt(whole(squares)) + NORM_EPS)
    for j, out in zip(BACK, outs):
        at = pl.ds(pl.multiple_of((shard ^ j) * rows, rows), rows)
        out[:rows] = graft * dir_ref[at, lane_tile(3 * chip + 2 * core)]
        out[rows:] = graft * fold(dir_ref[at, lane_tile(3 * chip + 1)], core)


def stats_kernel(tiles, shards, owner_ref, ah_ref, al_ref, bh_ref, bl_ref, ch_ref, cl_ref, left_ref, right_ref, nl_ref, nr_ref, gh_ref, gl_ref):
    shard, t, chip, core = place()
    rows = left_ref.shape[1]
    half = ah_ref.shape[0]
    side = shard // (shards // 2)

    def part(index):
        return pl.ds(pl.multiple_of(index * half, half), half)

    for ref, a, b, c in ((gh_ref, ah_ref, bh_ref, ch_ref), (gl_ref, al_ref, bl_ref, cl_ref)):
        ref[part(side), :] = a[...]
        ref[part(1 - side), part(chip)] = b[...]
        ref[part(1 - side), part(1 - chip)] = c[...]
    held = owner_ref[0] == shard
    for i in range(1, tiles):
        held = jnp.logical_or(held, owner_ref[i] == shard)

    def three(high, low, dims):
        dot = functools.partial(lax.dot_general, dimension_numbers=(dims, ((), ())), preferred_element_type=F32)
        return dot(high, gh_ref[...]) + dot(high, gl_ref[...]) + dot(low, gh_ref[...])

    def refreshed(old, new):
        return STAT_DECAY * old + (1.0 - STAT_DECAY) * jnp.where(held, new, 0.0)

    at = pl.ds(pl.multiple_of(t * rows, rows), rows)
    nl_ref[0] = refreshed(left_ref[0], three(gh_ref[at, :], gl_ref[at, :], ((1,), (1,))))
    end, mid = lane_tile(3 * chip + 2 * core), lane_tile(3 * chip + 1)
    ends = three(gh_ref[:, end], gl_ref[:, end], ((0,), (0,)))
    mids = three(gh_ref[:, mid], gl_ref[:, mid], ((0,), (0,)))
    half = LANES // 2

    @pl.when(core == 0)
    def _():
        nr_ref[0, :LANES] = refreshed(right_ref[0, :LANES], ends)
        nr_ref[0, LANES:] = refreshed(right_ref[0, LANES:], mids[:half])

    @pl.when(core == 1)
    def _():
        nr_ref[0, :half] = refreshed(right_ref[0, :half], mids[half:])
        nr_ref[0, half:] = refreshed(right_ref[0, half:], ends)


def back_kernel(rows, tiles, shards, owner_ref, *refs):
    blocks, out_ref = refs[:shards], refs[shards]
    shard, _, _, core = place()
    for j, block in zip(BACK, blocks):
        k = tile_of(owner_ref, shard ^ j, tiles)

        @pl.when(owner_ref[k] == (shard ^ j))
        def _(k=k, block=block):
            out_ref[k, :, :LANES], out_ref[k, :, LANES:] = unfold(block[...], rows, core)


def shape(dims, dtype=F32):
    return jax.ShapeDtypeStruct(dims, dtype)


def kernel_call(body, outs, ins, scratch=(), smem=0, flops=0, mib=16):
    vmem = pl.BlockSpec(memory_space=pltpu.VMEM)
    moved = sum(a.size * a.dtype.itemsize for a in (*ins, *jax.tree.leaves(outs)))
    return pl.pallas_call(
        body,
        out_shape=outs,
        in_specs=[pl.BlockSpec(memory_space=pltpu.SMEM)] * smem + [vmem] * (len(ins) - smem),
        out_specs=jax.tree.map(lambda _: vmem, outs),
        scratch_shapes=list(scratch),
        compiler_params=pltpu.CompilerParams(vmem_limit_bytes=mib << 20),
        cost_estimate=pl.CostEstimate(flops=flops, bytes_accessed=moved, transcendentals=0),
    )(*ins)


def swap(a, axis, mask):
    return lax.ppermute(a, axis, [(i, i ^ mask) for i in range(lax.axis_size(axis))])


def local(
    grad_parts, adam_v, left_stat, right_stat, left_root, right_root, owner, vec_parts, vec_m, vec_v
):
    shards = lax.axis_size("shard")
    tiles, rows, cols = adam_v.shape
    size = grad_parts.shape[3]
    packed = rows + rows // 2

    block = shape((tiles * packed, LANES))
    wide = shape((tiles * packed + EXTRA, LANES))
    sf, kf = kernel_call(functools.partial(split_kernel, rows, tiles, True), (block, block), (grad_parts,))
    sn, kn = kernel_call(functools.partial(split_kernel, rows, tiles, False), (wide, wide), (grad_parts, vec_parts))
    u = kf + swap(sf, "tensor", 1)
    rn = swap(sn, "tensor", 1)
    r = swap(u, "tensor", 2)
    roots = jnp.concatenate([left_root, right_root], axis=0)
    quadrant = lax.axis_index("tensor") // 2 * (size // 2)
    crossing = lax.dynamic_slice_in_dim(roots, quadrant, size // 2, 2)
    roots_core = swap(roots, "tensor", 1)
    r, roots, roots_core, crossing = lax.optimization_barrier((r, roots, roots_core, crossing))
    res = kernel_call(
        functools.partial(adam_kernel, rows, tiles, shards),
        (shape((packed + EXTRA, LANES)),) * shards + (shape(adam_v.shape), shape((EXTRA, LANES))),
        (owner, kn, rn, r, adam_v),
        (pltpu.VMEM((tiles, packed, LANES), F32), pltpu.VMEM((tiles, EXTRA, LANES), F32)),
        smem=1,
    )
    outgoing, (adam_new, vec_pair) = res[:shards], res[shards:]

    arrived = [outgoing[0]] + [swap(outgoing[j], "shard", j) for j in range(1, shards)]
    crossing, vec_pair = lax.optimization_barrier((crossing, vec_pair))
    roots_chip = swap(crossing, "tensor", 2)
    near = jnp.concatenate([*arrived[: shards // 2], vec_pair], axis=0)
    far = jnp.concatenate(arrived[shards // 2 :], axis=0)
    near, roots_chip = lax.optimization_barrier((near, roots_chip))
    near_across = swap(near, "tensor", 2)
    near_across, roots_both = lax.optimization_barrier((near_across, swap(roots_chip, "tensor", 1)))
    full = shape((size, size), BF16)
    left_full, right_full = kernel_call(
        roots_kernel, (full, full), (roots, roots_core, roots_chip, roots_both), mib=24
    )
    near = near, swap(near, "tensor", 1), near_across, swap(near_across, "tensor", 1)
    far_across = swap(far, "tensor", 2)
    half = size // 2
    tall, square = shape((half, size), BF16), shape((half, half), BF16)
    vec = shape(vec_m.shape)
    ah, al, bh, bl, z, part, adam, new_vec_m, new_vec_v, vec_step, new_adam_v = kernel_call(
        functools.partial(near_kernel, rows, shards),
        (tall, tall, square, square, shape((half, size)), shape((size, size)), shape((EXTRA, LANES)), vec, vec, vec, shape(adam_v.shape)),
        (*near, far, swap(far, "tensor", 1), left_full, right_full, vec_m, vec_v, adam_new),
        (pltpu.VMEM((half, size), BF16),) * 2,
        flops=5 * size**3,
        mib=32,
    )
    far_across, adam = lax.optimization_barrier((far_across, adam))
    ch, cl, *ready = kernel_call(
        functools.partial(owner_kernel, rows, shards),
        (square, square) + (shape((packed, LANES)),) * shards,
        (far_across, swap(far_across, "tensor", 1), z, part, adam, left_full, right_full),
        (pltpu.VMEM((half, size), BF16),) * 2 + (pltpu.VMEM((size, size), F32),),
        flops=3 * size**3,
        mib=32,
    )
    back = [swap(block, "shard", j) if j else block for j, block in zip(BACK, ready)]
    new_left, new_right = kernel_call(
        functools.partial(stats_kernel, tiles, shards),
        (shape(left_stat.shape), shape(right_stat.shape)),
        (owner, ah, al, bh, bl, ch, cl, left_stat, right_stat),
        (pltpu.VMEM((size, size), BF16),) * 2,
        smem=1,
        flops=12 * cols * size**2,
        mib=32,
    )
    update = kernel_call(
        functools.partial(back_kernel, rows, tiles, shards), shape(adam_v.shape), (owner, *back), smem=1
    )
    return (update, new_adam_v, new_left, new_right, new_vec_m, new_vec_v, vec_step)


def solution(mesh):
    in_specs = (
        P("tensor", None, "shard", None),
        P(None, "shard", "tensor"),
        P("shard", "tensor", None),
        P("shard", "tensor", None),
        P("shard", "tensor", None),
        P("shard", "tensor", None),
        P(),
        P("tensor", None, "shard"),
        P(None, "shard"),
        P(None, "shard"),
    )
    out_specs = (
        P(None, "shard", "tensor"),
        P(None, "shard", "tensor"),
        P("shard", "tensor", None),
        P("shard", "tensor", None),
        P(None, "shard"),
        P(None, "shard"),
        P(None, "shard"),
    )
    packs = mesh.shape["tensor"] == 4 and mesh.shape["shard"] == 8
    return jax.shard_map(
        local if packs else plain, mesh=mesh, in_specs=in_specs, out_specs=out_specs, check_vma=False
    )
```
